32 devices in a mesh: rows: 8 (over z, y), cols: 4 (over x, core).
Axes of the slice: x: 2, y: 2, z: 4, core: 2. Of those that a mesh axis runs over, the one named last changes fastest.
Arguments:
- tokens: bfloat16 [96, 96, 768], P('rows', 'cols'), may hold values from -48 to 48
- ln_gain: float32 [768], replicated, may hold values from 0.5 to 1.5
- ln_bias: float32 [768], replicated, may hold values from -3 to 3
- qkv_weight: bfloat16 [768, 2304], replicated, may hold values from -3 to 3
- qkv_bias: float32 [2304], replicated, may hold values from -3 to 3
- rel_table: float32 [23, 23, 24], replicated, may hold values from -4 to 4
- proj_weight: bfloat16 [768, 768], replicated, may hold values from -0.21875 to 0.21875
- proj_bias: float32 [768], replicated, may hold values from -3 to 3
- branch_weight: bfloat16 [4, 768, 512], replicated, may hold values from -0.21875 to 0.21875
- branch_bias: float32 [4, 512], replicated, may hold values from -4 to 4
- join_block: bfloat16 [768, 512], replicated, may hold values from -0.109375 to 0.109375
- join_branch: bfloat16 [4, 512, 512], replicated, may hold values from -0.375 to 0.375
- bn_gain: float32 [512], replicated, may hold values from 0.25 to 1.75
- bn_bias: float32 [512], replicated, may hold values from -4 to 4
Outputs:
- joined: bfloat16 [96, 96, 512], P('rows', 'cols')
The draws below stay inside these ranges and needn't reach their ends.
All inputs are finite; a program needn't handle non-finite values.
Results may differ from the reference program's by a relative error of at most 0.0049.
Values may be sent and summed in bfloat16 or wider, within the bound.
No kernel may reach another device: no remote copies, remote signals or barrier semaphores. Data moves between devices by JAX's collectives and lax.ppermute only.
A program may use at most 128 MiB of HBM per device.

```python
import math
import jax
import jax.numpy as jnp
from jax import lax

D = 768
HEADS = 24
CH = 512
WIN = 12
HEIGHT = 96
WIDTH = 96


def draw_tokens(key, part):
    subkeys = jax.random.split(jax.random.fold_in(key, 11), 10)
    row_index = jnp.arange(HEIGHT, dtype=jnp.int32)
    row_frac = row_index.astype(jnp.float32)[:, None, None] / HEIGHT
    col_frac = jnp.arange(WIDTH, dtype=jnp.float32)[None, :, None] / WIDTH
    coarse = jax.random.truncated_normal(subkeys[1], -3.0, 3.0, (HEIGHT // 4, WIDTH // 4, D), jnp.float32)
    coarse = jnp.repeat(jnp.repeat(coarse, 4, axis=0), 4, axis=1)
    row_slope = jax.random.truncated_normal(subkeys[2], -3.0, 3.0, (D,), jnp.float32)
    col_tilt = jax.random.truncated_normal(subkeys[3], -3.0, 3.0, (D,), jnp.float32)
    trend_part = row_slope * (1.0 + 2.0 * row_frac) + 0.5 * col_tilt * col_frac
    band_rows = 4 * WIN
    band_count = HEIGHT // band_rows + 1
    band_levels = jnp.exp(jax.random.uniform(subkeys[5], (band_count,), jnp.float32, math.log(1.0 / 3.0), math.log(3.0)))
    band_onehot = (row_index[:, None] // band_rows == jnp.arange(band_count, dtype=jnp.int32)[None, :]).astype(jnp.float32)
    band_factor = jnp.sum(band_onehot * band_levels[None, :], 1)[:, None, None]
    row_amp = jax.random.uniform(subkeys[6], (D,), jnp.float32, 0.5, 1.0)
    col_amp = jax.random.uniform(subkeys[7], (D,), jnp.float32, 0.5, 1.0)
    row_phase = jax.random.uniform(subkeys[8], (D,), jnp.float32, 0.0, 2.0 * math.pi)
    col_phase = jax.random.uniform(subkeys[9], (D,), jnp.float32, 0.0, 2.0 * math.pi)
    smooth_part = 8.0 * row_amp * jnp.cos(6.0 * math.pi * row_frac + row_phase) + 4.0 * col_amp * jnp.cos(6.0 * math.pi * col_frac + col_phase)
    noise_part = jax.random.truncated_normal(subkeys[0], -3.0, 3.0, (HEIGHT, WIDTH, D), jnp.float32)
    values = band_factor * (0.8 * noise_part + 0.6 * coarse) + trend_part + smooth_part
    values = jnp.clip(values, -47.5, 47.5)
    return values.astype(jnp.bfloat16)


def draw_qkv_weight(key, part):
    base = jax.random.truncated_normal(jax.random.fold_in(key, 23), -3.0, 3.0, (D, 3 * D), jnp.float32) / math.sqrt(D)
    return base.astype(jnp.bfloat16)


def bell_draw(stream_key, dims, scale, most, kind=jnp.bfloat16):
    return jnp.clip(scale * jax.random.normal(stream_key, dims, jnp.float32), -most, most).astype(kind)


def setup_inputs(seed: int = 0) -> dict:
    arg_keys = jax.random.split(jax.random.key(seed), 15)
    tokens = draw_tokens(jax.random.fold_in(arg_keys[14], 71), 0)
    ln_gain = jnp.clip(1.0 + 0.1 * jax.random.normal(arg_keys[1], (D,), jnp.float32), 0.5, 1.5)
    ln_bias = bell_draw(arg_keys[2], (D,), 0.5, 3.0, jnp.float32)
    qkv_weight = draw_qkv_weight(jax.random.fold_in(arg_keys[14], 71), 0)
    qkv_bias = bell_draw(arg_keys[4], (3 * D,), 0.5, 3.0, jnp.float32)
    rel_table = bell_draw(arg_keys[5], (2 * WIN - 1, 2 * WIN - 1, HEADS), 1.0, 4.0, jnp.float32)
    proj_weight = bell_draw(arg_keys[6], (D, D), D ** -0.5, 0.21875)
    proj_bias = bell_draw(arg_keys[7], (D,), 0.5, 3.0, jnp.float32)
    branch_weight = bell_draw(arg_keys[8], (4, D, CH), D ** -0.5, 0.21875)
    branch_bias = bell_draw(arg_keys[9], (4, CH), 1.0, 4.0, jnp.float32)
    join_block = bell_draw(arg_keys[10], (D, CH), (D + 4 * CH) ** -0.5, 0.109375)
    join_branch = bell_draw(arg_keys[11], (4, CH, CH), (CH // 2) ** -0.5, 0.375)
    bn_gain = jnp.clip(1.0 + 0.15 * jax.random.normal(arg_keys[12], (CH,), jnp.float32), 0.25, 1.75)
    bn_bias = bell_draw(arg_keys[13], (CH,), 1.0, 4.0, jnp.float32)
    return {"tokens": tokens, "ln_gain": ln_gain, "ln_bias": ln_bias, "qkv_weight": qkv_weight, "qkv_bias": qkv_bias, "rel_table": rel_table, "proj_weight": proj_weight, "proj_bias": proj_bias, "branch_weight": branch_weight, "branch_bias": branch_bias, "join_block": join_block, "join_branch": join_branch, "bn_gain": bn_gain, "bn_bias": bn_bias}


bin_scales = (1, 2, 3, 6)
bin_starts = (0, 1, 3, 6)
norm_eps = 1e-05
highest = lax.Precision.HIGHEST

def layer_norm(values, norm_gain, norm_bias):
    floats = values.astype(jnp.float32)
    center = lax.optimization_barrier(jnp.mean(floats, -1, keepdims=True))
    spread_sq = lax.optimization_barrier(jnp.mean(jnp.square(floats - center), -1, keepdims=True))
    return ((floats - center) * lax.rsqrt(spread_sq + norm_eps) * norm_gain + norm_bias).astype(jnp.bfloat16)

def relative_bias(rel_table):
    steps_idx = jnp.arange(WIN, dtype=jnp.int32)
    offsets = steps_idx[:, None] - steps_idx[None, :] + WIN - 1
    onehot = (offsets[:, :, None] == jnp.arange(2 * WIN - 1, dtype=jnp.int32)[None, None, :]).astype(jnp.float32)
    pair_bias = jnp.einsum('pra,qsb,abh->hpqrs', onehot, onehot, rel_table, precision=highest)
    return pair_bias.reshape(rel_table.shape[2], WIN * WIN, WIN * WIN)

def region_labels(positions, total):
    return (positions >= total - WIN).astype(jnp.int32) + (positions >= total - WIN // 2).astype(jnp.int32)

def window_mask(row_place, col_place, height, breadth):
    labels = 3 * region_labels(row_place, height)[:, None] + region_labels(col_place, breadth)[None, :]
    labels = labels.reshape(row_place.shape[0] // WIN, WIN, col_place.shape[0] // WIN, WIN)
    labels = labels.transpose(0, 2, 1, 3).reshape(-1, WIN * WIN)
    return jnp.where(labels[:, :, None] != labels[:, None, :], -100.0, 0.0).astype(jnp.float32)

def window_attention(normed, qkv_weight, qkv_bias, proj_weight, proj_bias, pair_bias, mask_add):
    row_count, col_count, width = normed.shape
    heads_count = pair_bias.shape[0]
    head_size = width // heads_count
    windows = normed.reshape(row_count // WIN, WIN, col_count // WIN, WIN, width)
    windows = windows.transpose(0, 2, 1, 3, 4).reshape(-1, WIN * WIN, width)
    count_win = windows.shape[0]
    mixed = jnp.dot(windows.reshape(-1, width), qkv_weight, preferred_element_type=jnp.float32) + qkv_bias
    mixed = mixed.reshape(count_win, WIN * WIN, 3, heads_count, head_size)
    queries = (mixed[:, :, 0] * head_size ** (-0.5)).astype(jnp.bfloat16)
    keys_bf = mixed[:, :, 1].astype(jnp.bfloat16)
    values_bf = mixed[:, :, 2].astype(jnp.bfloat16)
    scores = jnp.einsum('wihd,wjhd->whij', queries.astype(jnp.float32), keys_bf.astype(jnp.float32))
    scores = scores + pair_bias[None] + mask_add[:, None]
    weights = jax.nn.softmax(scores, axis=-1).astype(jnp.bfloat16)
    context = jnp.einsum('whij,wjhd->wihd', weights.astype(jnp.float32), values_bf.astype(jnp.float32))
    context = context.astype(jnp.bfloat16).reshape(-1, width)
    output = jnp.dot(context, proj_weight, preferred_element_type=jnp.float32) + proj_bias
    output = output.reshape(row_count // WIN, col_count // WIN, WIN, WIN, width).transpose(0, 2, 1, 3, 4)
    return output.reshape(row_count, col_count, width)

def bin_tables(positions, total):
    pooling = []
    spread = []
    place_f = positions.astype(jnp.float32)
    for scale_value in bin_scales:
        levels = jnp.arange(scale_value, dtype=jnp.int32)
        pooling.append((positions[:, None] // (total // scale_value) == levels[None, :]).astype(jnp.float32))
        source = jnp.clip((place_f + 0.5) * (scale_value / total) - 0.5, 0.0, scale_value - 1.0)
        spread.append(jax.nn.relu(1.0 - jnp.abs(source[:, None] - levels[None, :].astype(jnp.float32))))
    return (jnp.concatenate(pooling, 1), jnp.concatenate(spread, 1))

def branch_projections(pooled, branch_weight, branch_bias, join_branch):
    results = []
    start_row = 0
    for branch_index, scale_value in enumerate(bin_scales):
        cell_rows = pooled[start_row:start_row + scale_value * scale_value]
        hidden_map = jax.nn.relu(jnp.dot(cell_rows, branch_weight[branch_index].astype(jnp.float32), precision=highest) + branch_bias[branch_index])
        results.append(jnp.dot(hidden_map, join_branch[branch_index].astype(jnp.float32), precision=highest))
        start_row += scale_value * scale_value
    return jnp.concatenate(results, 0)

def spread_cells(projected, row_spread, col_spread):
    total_map = jnp.zeros((row_spread.shape[0], col_spread.shape[0], projected.shape[1]), jnp.float32)
    start_row = 0
    for scale_value, start_value in zip(bin_scales, bin_starts):
        block_cells = projected[start_row:start_row + scale_value * scale_value].reshape(scale_value, scale_value, -1)
        across = jnp.einsum('cb,abh->ach', col_spread[:, start_value:start_value + scale_value], block_cells, precision=highest)
        total_map = total_map + jnp.einsum('ra,ach->rch', row_spread[:, start_value:start_value + scale_value], across, precision=highest)
        start_row += scale_value * scale_value
    return total_map

def reference(tokens, ln_gain, ln_bias, qkv_weight, qkv_bias, rel_table, proj_weight, proj_bias, branch_weight, branch_bias, join_block, join_branch, bn_gain, bn_bias):
    half = WIN // 2
    rolled_tok = jnp.roll(tokens, (-half, -half), (0, 1))
    normed = layer_norm(rolled_tok, ln_gain, ln_bias)
    pair_bias = relative_bias(rel_table)
    col_place = jnp.arange(WIDTH, dtype=jnp.int32)

    def one_strip(start_row):
        strip = lax.dynamic_slice_in_dim(normed, start_row, WIN, 0)
        row_place = start_row + jnp.arange(WIN, dtype=jnp.int32)
        mask_add = window_mask(row_place, col_place, HEIGHT, WIDTH)
        return window_attention(strip, qkv_weight, qkv_bias, proj_weight, proj_bias, pair_bias, mask_add)
    starts = (jnp.arange(HEIGHT // WIN, dtype=jnp.int32) * WIN).astype(jnp.int32)
    attended = lax.map(one_strip, starts).reshape(HEIGHT, WIDTH, D)
    block_out = (rolled_tok.astype(jnp.float32) + attended).astype(jnp.bfloat16)
    block_out = jnp.roll(block_out, (half, half), (0, 1))
    floats = block_out.astype(jnp.float32)
    pieces = []
    for scale_value in bin_scales:
        cell_mean = floats.reshape(scale_value, HEIGHT // scale_value, scale_value, WIDTH // scale_value, D).mean(axis=(1, 3))
        pieces.append(cell_mean.reshape(scale_value * scale_value, D))
    projected = branch_projections(jnp.concatenate(pieces, 0), branch_weight, branch_bias, join_branch)
    row_spread = bin_tables(jnp.arange(HEIGHT, dtype=jnp.int32), HEIGHT)[1]
    col_spread = bin_tables(jnp.arange(WIDTH, dtype=jnp.int32), WIDTH)[1]
    direct = jnp.dot(block_out.reshape(-1, D), join_block, preferred_element_type=jnp.float32).reshape(HEIGHT, WIDTH, CH)
    pre_norm = direct + spread_cells(projected, row_spread, col_spread)
    mean_val = lax.optimization_barrier(jnp.mean(pre_norm, axis=(0, 1)))
    variance = lax.optimization_barrier(jnp.mean(jnp.square(pre_norm - mean_val), axis=(0, 1)))
    joined = jax.nn.relu((pre_norm - mean_val) * lax.rsqrt(variance + norm_eps) * bn_gain + bn_bias)
    return joined.astype(jnp.bfloat16)
```

```python
import functools

import jax
import jax.numpy as jnp
import numpy as np
from jax import lax
from jax.experimental import pallas as pl
from jax.experimental.pallas import tpu as pltpu
from jax.sharding import PartitionSpec as P

WIN = 12
HALF = WIN // 2
bin_scales = (1, 2, 3, 6)
norm_eps = 1e-05
highest = lax.Precision.HIGHEST
f32 = jnp.float32
bf16 = jnp.bfloat16
axes = ("rows", "cols")


def up(count, step):
    return -(-count // step) * step


def window_order(row_count, col_count):
    order = []
    for wr in range(row_count // WIN):
        for wc in range(col_count // WIN):
            for p in range(WIN):
                for q in range(WIN):
                    order.append((wr * WIN + p, wc * WIN + q))
    return order


def piece_sizes(row_count, col_count):
    inner_r, inner_c = row_count - HALF, col_count - HALF
    sizes = [inner_r * inner_c, HALF * inner_c, inner_r * HALF, HALF * HALF]
    starts, at = [], 0
    for size in sizes:
        starts.append(at)
        at += up(size, 16)
    return sizes, starts, at


def roll_gather(row_count, col_count):
    inner_r, inner_c = row_count - HALF, col_count - HALF
    _, starts, total = piece_sizes(row_count, col_count)
    table = np.zeros((row_count * col_count, total), np.float32)
    for token, (i, j) in enumerate(window_order(row_count, col_count)):
        if i < inner_r and j < inner_c:
            source = starts[0] + i * inner_c + j
        elif j < inner_c:
            source = starts[1] + (i - inner_r) * inner_c + j
        elif i < inner_r:
            source = starts[2] + i * HALF + (j - inner_c)
        else:
            source = starts[3] + (i - inner_r) * HALF + (j - inner_c)
        table[token, source] = 1.0
    return table


def unroll_scatter(row_count, col_count):
    inner_r, inner_c = row_count - HALF, col_count - HALF
    _, starts, total = piece_sizes(row_count, col_count)
    table = np.zeros((total, row_count * col_count), np.float32)
    for token, (i, j) in enumerate(window_order(row_count, col_count)):
        if i < inner_r and j < inner_c:
            target = starts[0] + i * inner_c + j
        elif j < inner_c:
            target = starts[1] + (i - inner_r) * inner_c + j
        elif i < inner_r:
            target = starts[2] + i * HALF + (j - inner_c)
        else:
            target = starts[3] + (i - inner_r) * HALF + (j - inner_c)
        table[target, token] = 1.0
    return table


def unroll_gather(row_count, col_count):
    inner_c = col_count - HALF
    _, starts, total = piece_sizes(row_count, col_count)
    table = np.zeros((row_count * col_count, total), np.float32)
    for i in range(row_count):
        for j in range(col_count):
            if i >= HALF and j >= HALF:
                source = starts[0] + (i - HALF) * inner_c + (j - HALF)
            elif j >= HALF:
                source = starts[1] + i * inner_c + (j - HALF)
            elif i >= HALF:
                source = starts[2] + (i - HALF) * HALF + j
            else:
                source = starts[3] + i * HALF + j
            table[i * col_count + j, source] = 1.0
    return table


def cell_list():
    cells = []
    for s in bin_scales:
        for a in range(s):
            for b in range(s):
                cells.append((s, a, b))
    return cells


CELLS = cell_list()
NCELL = len(CELLS)
FINE = bin_scales[-1]
NFINE = FINE * FINE
CELL_PAD = up(NCELL + 1, 8)
FINE_PAD = up(NFINE, 8)


def cell_table(height, breadth):
    table = np.zeros((64, 8), np.float32)
    for k, (s, a, b) in enumerate(CELLS):
        table[k, :5] = (s / height, s / breadth, s - 1.0, a, b)
    table[NCELL:, 3] = -9.0
    return table


def fine_table(height, breadth):
    table = np.zeros((FINE_PAD, 8), np.float32)
    table[:, :4] = -1.0
    for a in range(FINE):
        for b in range(FINE):
            table[a * FINE + b, :4] = (
                a * (height // FINE),
                (a + 1) * (height // FINE),
                b * (breadth // FINE),
                (b + 1) * (breadth // FINE),
            )
    return table


def group_table():
    table = np.zeros((64, FINE_PAD), np.float32)
    for k, (s, a, b) in enumerate(CELLS):
        step = FINE // s
        for aa in range(a * step, (a + 1) * step):
            for bb in range(b * step, (b + 1) * step):
                table[k, aa * FINE + bb] = 1.0
    return table


def spread_weights(total, s):
    place = np.clip((np.arange(total) + 0.5) * s / total - 0.5, 0.0, s - 1.0)
    return np.maximum(0.0, 1.0 - np.abs(place[:, None] - np.arange(s)[None, :]))


def gram_tables(height, breadth):
    rows = np.zeros((height, 64))
    cols = np.zeros((breadth, 64))
    for k, (s, a, b) in enumerate(CELLS):
        rows[:, k] = spread_weights(height, s)[:, a]
        cols[:, k] = spread_weights(breadth, s)[:, b]
    gram = (rows.T @ rows) * (cols.T @ cols)
    mass = rows.sum(0) * cols.sum(0)
    gram[NCELL] = mass
    return gram.astype(np.float32)


def bias_kernel(rel_ref, out_ref, g_ref):
    heads = rel_ref.shape[0]
    span = 2 * WIN - 1
    lane = lax.broadcasted_iota(jnp.int32, (heads, 16, 128), 2)
    tiles = [jnp.zeros((heads, 16, 128), f32) for _ in range(3)]
    for a in range(span):
        line = rel_ref[:, a : a + 1, :]
        shift = (WIN * a - (WIN - 1)) % 128
        if shift > 112:
            line = pltpu.roll(line, shift, 2)
            shift = 0
        line = jnp.broadcast_to(line, (heads, 16, 128))
        moved = pltpu.roll(line, shift, 2, stride=1, stride_axis=1)
        first, last = WIN * a, WIN * a + WIN
        for t in range(first // 128, (last - 1) // 128 + 1):
            inside = (lane >= first - 128 * t) & (lane < last - 128 * t)
            tiles[t] = jnp.where(inside, moved, tiles[t])
    for t in range(3):
        g_ref[:, :, 128 * t : 128 * t + 128] = tiles[t]
    for u in range(WIN):
        offset = WIN * (WIN - 1 - u)
        wide = g_ref[...]
        if offset:
            wide = pltpu.roll(wide, 384 - offset, 2)
        out_ref[:, WIN * u : WIN * u + WIN, :] = wide[:, :WIN, : WIN * WIN]


def expanded_bias(rel_table):
    heads = rel_table.shape[2]
    span = 2 * WIN - 1
    rel = jnp.transpose(rel_table, (2, 0, 1))
    rel = jnp.pad(rel, ((0, 0), (0, 24 - span), (0, 128 - span)))
    tokens = WIN * WIN
    return pl.pallas_call(
        bias_kernel,
        out_shape=jax.ShapeDtypeStruct((heads, tokens, tokens), f32),
        in_specs=[pl.BlockSpec(memory_space=pltpu.VMEM)],
        out_specs=pl.BlockSpec(memory_space=pltpu.VMEM),
        scratch_shapes=[pltpu.VMEM((heads, 16, 384), f32)],
        compiler_params=pltpu.CompilerParams(vmem_limit_bytes=16 << 20),
        cost_estimate=pl.CostEstimate(
            flops=4 * heads * tokens * tokens,
            bytes_accessed=4 * heads * tokens * 256,
            transcendentals=0,
        ),
        name="expand_bias",
    )(rel)


def contract(a, b, dims, **kw):
    return lax.dot_general(a, b, (dims, ((), ())), preferred_element_type=f32, **kw)


def attention_kernel(
    geo,
    place_ref,
    own_ref,
    rr_ref,
    rc_ref,
    rd_ref,
    gather_ref,
    scatter_ref,
    lng_ref,
    lnb_ref,
    wqkv_ref,
    bqkv_ref,
    bias_ref,
    wproj_ref,
    bproj_ref,
    wjoin_ref,
    token_ref,
    cell_ref,
    fine_ref,
    keep_ref,
    send_ref,
    o_own_ref,
    o_row_ref,
    o_col_ref,
    o_diag_ref,
    xs_ref,
    q_ref,
    k_ref,
    vt_ref,
    ct_ref,
    blk_ref,
    pen_ref,
    buf_ref,
):
    row_count, col_count, height, breadth = geo
    nwr, nwc = row_count // WIN, col_count // WIN
    tokens, width = row_count * col_count, own_ref.shape[1]
    wt = WIN * WIN
    heads = bias_ref.shape[0]
    hd = width // heads
    per_tile = 128 // hd
    sizes, starts, total = piece_sizes(row_count, col_count)
    my_row, my_col, bit = place_ref[0], place_ref[1], place_ref[2]

    xs_ref[...] = jnp.zeros_like(xs_ref)
    for ref, start, size in zip((own_ref, rr_ref, rc_ref, rd_ref), starts, sizes):
        xs_ref[start : start + size, :] = ref[...]
    rolled = contract(gather_ref[...], xs_ref[...], ((1,), (0,)))
    center = jnp.mean(rolled, -1, keepdims=True)
    delta = rolled - center
    spread = jnp.mean(delta * delta, -1, keepdims=True)
    normed = (delta * lax.rsqrt(spread + norm_eps) * lng_ref[...] + lnb_ref[...]).astype(bf16)
    blk_ref[...] = rolled.astype(bf16)
    for part in range(3):
        cols = slice(part * width, (part + 1) * width)
        mixed = contract(normed, wqkv_ref[:, cols], ((1,), (0,))) + bqkv_ref[:, cols]
        if part == 0:
            q_ref[...] = (mixed * hd ** (-0.5)).astype(bf16).reshape(q_ref.shape)
        elif part == 1:
            k_ref[...] = mixed.astype(bf16).reshape(k_ref.shape)
        else:
            for w in range(nwr * nwc):
                vt_ref[w] = mixed[w * wt : (w + 1) * wt].T.astype(bf16)

    sub = lax.broadcasted_iota(jnp.int32, (wt, wt), 0)
    lane = lax.broadcasted_iota(jnp.int32, (wt, wt), 1)
    row_diff = (sub < wt // 2) != (lane < wt // 2)
    col_diff = (sub % WIN < HALF) != (lane % WIN < HALF)
    for wr in range(nwr):
        for wc in range(nwc):
            row_last = my_row * nwr + wr == height // WIN - 1
            col_last = my_col * nwc + wc == breadth // WIN - 1
            bad = (row_diff & row_last) | (col_diff & col_last)
            pen_ref[wr * nwc + wc] = jnp.where(bad, -100.0, 0.0)

    head_lane = lax.broadcasted_iota(jnp.int32, (wt, 128), 1) // hd

    def tile_step(step, carry):
        w = step // (width // 128)
        t = step % (width // 128)
        at = pl.multiple_of(t * 128, 128)
        queries = q_ref[w, :, pl.ds(at, 128)]
        keys = k_ref[w, :, pl.ds(at, 128)]
        pen = pen_ref[w]
        for hh in range(per_tile):
            keys_h = jnp.where(head_lane == hh, keys, jnp.zeros_like(keys))
            scores = contract(keys_h, queries, ((1,), (1,)))
            scores = scores + bias_ref[t * per_tile + hh] + pen
            top = jnp.max(scores, 0, keepdims=True)
            grown = jnp.exp(scores - top)
            weights = (grown * (1.0 / jnp.sum(grown, 0, keepdims=True))).astype(bf16)
            place = pl.multiple_of(at + hh * hd, hd)
            context = contract(vt_ref[w, pl.ds(place, hd), :], weights, ((1,), (0,)))
            ct_ref[w, pl.ds(place, hd), :] = context.astype(bf16)
        return carry

    lax.fori_loop(0, nwr * nwc * (width // 128), tile_step, 0)

    for w in range(nwr * nwc):
        attended = contract(ct_ref[w], wproj_ref[...], ((0,), (0,))) + bproj_ref[...]
        here = slice(w * wt, (w + 1) * wt)
        blk_ref[here, :] = (blk_ref[here, :].astype(f32) + attended).astype(bf16)

    block = blk_ref[...]
    pieces = contract(scatter_ref[...], block, ((1,), (0,))).astype(bf16)
    for ref, start, size in zip((o_own_ref, o_row_ref, o_col_ref, o_diag_ref), starts, sizes):
        ref[...] = pieces[start : start + size]

    row = token_ref[0:1, :] + (my_row * row_count + HALF).astype(f32)
    col = token_ref[1:2, :] + (my_col * col_count + HALF).astype(f32)
    row = jnp.where(row >= height, row - height, row)
    col = jnp.where(col >= breadth, col - breadth, col)
    fine = fine_ref[...]
    inside = (
        (row >= fine[:, 0:1]) & (row < fine[:, 1:2]) & (col >= fine[:, 2:3]) & (col < fine[:, 3:4])
    )
    pooled = contract(inside.astype(bf16), block, ((1,), (0,)))
    cell = cell_ref[:CELL_PAD, :]
    row_at = jnp.clip((row + 0.5) * cell[:, 0:1] - 0.5, 0.0, cell[:, 2:3])
    col_at = jnp.clip((col + 0.5) * cell[:, 1:2] - 0.5, 0.0, cell[:, 2:3])
    share = jnp.maximum(0.0, 1.0 - jnp.abs(row_at - cell[:, 3:4])) * jnp.maximum(
        0.0, 1.0 - jnp.abs(col_at - cell[:, 4:5])
    )
    direct = contract(block, wjoin_ref[...], ((1,), (0,)))
    weighted = contract(share, direct, ((1,), (0,)), precision=highest)
    squares = jnp.sum(direct * direct, 0, keepdims=True)
    which = lax.broadcasted_iota(jnp.int32, weighted.shape, 0)
    weighted = jnp.where(which == NCELL, squares, weighted)
    half_w, half_c = width // 2, direct.shape[1] // 2
    for b in range(2):
        at = 0
        for t in range(half_w // 128):
            lo = b * half_w + t * 128
            buf_ref[b, at : at + FINE_PAD, :] = pooled[:, lo : lo + 128]
            at += FINE_PAD
        for t in range(half_c // 128):
            lo = b * half_c + t * 128
            buf_ref[b, at : at + CELL_PAD, :] = weighted[:, lo : lo + 128]
            at += CELL_PAD
    keep_ref[...] = buf_ref[bit]
    send_ref[...] = buf_ref[1 - bit]


def half_rows(width, channels):
    return FINE_PAD * (width // 256) + CELL_PAD * (channels // 256)


def direct_kernel(
    geo, place_ref, own_ref, rr_ref, rc_ref, rd_ref, gather_ref, wjoin_ref, token_ref, cell_ref,
    out_ref, share_ref, xs_ref
):
    row_count, col_count, height, breadth = geo
    sizes, starts, total = piece_sizes(row_count, col_count)
    my_row, my_col = place_ref[0], place_ref[1]
    xs_ref[...] = jnp.zeros_like(xs_ref)
    for ref, start, size in zip((own_ref, rr_ref, rc_ref, rd_ref), starts, sizes):
        xs_ref[start : start + size, :] = ref[...]
    block = contract(gather_ref[...], xs_ref[...], ((1,), (0,))).astype(bf16)
    out_ref[...] = contract(block, wjoin_ref[...], ((1,), (0,)))
    row = token_ref[:, 0:1] + (my_row * row_count).astype(f32)
    col = token_ref[:, 1:2] + (my_col * col_count).astype(f32)
    row_at = jnp.clip((row + 0.5) * cell_ref[0:1, :] - 0.5, 0.0, cell_ref[2:3, :])
    col_at = jnp.clip((col + 0.5) * cell_ref[1:2, :] - 0.5, 0.0, cell_ref[2:3, :])
    share = jnp.maximum(0.0, 1.0 - jnp.abs(row_at - cell_ref[3:4, :])) * jnp.maximum(
        0.0, 1.0 - jnp.abs(col_at - cell_ref[4:5, :])
    )
    upper = share.astype(bf16)
    lower = (share - upper.astype(f32)).astype(bf16)
    lane = lax.broadcasted_iota(jnp.int32, share.shape, 1)
    share_ref[:, :128] = upper
    share_ref[:, 128:] = lower


def two_parts(value):
    upper = value.astype(bf16)
    return upper, (value - upper.astype(f32)).astype(bf16)


def final_kernel(
    geo,
    place_ref,
    mine_ref,
    other_ref,
    direct_ref,
    share_ref,
    wb_ref,
    bb_ref,
    jb_ref,
    group_ref,
    gram_ref,
    gain_ref,
    bias_ref,
    out_ref,
    buf_ref,
    pool_ref,
    wei_ref,
    proj_ref,
):
    row_count, col_count, height, breadth = geo
    bit = place_ref[2]
    width, channels = pool_ref.shape[1], wei_ref.shape[1]
    half_w, half_c = width // 2, channels // 2
    buf_ref[bit] = mine_ref[...]
    buf_ref[1 - bit] = other_ref[...]
    for b in range(2):
        at = 0
        for t in range(half_w // 128):
            lo = b * half_w + t * 128
            pool_ref[:, lo : lo + 128] = buf_ref[b, at : at + FINE_PAD, :]
            at += FINE_PAD
        for t in range(half_c // 128):
            lo = b * half_c + t * 128
            wei_ref[:, lo : lo + 128] = buf_ref[b, at : at + CELL_PAD, :]
            at += CELL_PAD
    cells = contract(group_ref[...], pool_ref[...], ((1,), (0,)), precision=highest)
    proj_ref[...] = jnp.zeros_like(proj_ref)
    start = 0
    for k, s in enumerate(bin_scales):
        count = s * s
        scale = 1.0 / float((height // s) * (breadth // s))
        upper, lower = two_parts(cells[start : start + count] * scale)
        hidden = contract(upper, wb_ref[k], ((1,), (0,))) + contract(lower, wb_ref[k], ((1,), (0,)))
        hidden = jnp.maximum(hidden + bb_ref[k : k + 1, :], 0.0)
        upper, lower = two_parts(hidden)
        proj_ref[start : start + count, :] = contract(upper, jb_ref[k], ((1,), (0,))) + contract(
            lower, jb_ref[k], ((1,), (0,))
        )
        start += count
    projected = proj_ref[...]
    everyone = float(height * breadth)
    spun = contract(gram_ref[...], projected, ((1,), (0,)), precision=highest)
    weighted = wei_ref[...]
    lifted_sum = spun[NCELL : NCELL + 1]
    mixed = projected[:NCELL] * (spun[:NCELL] + 2.0 * weighted[:NCELL])
    mean_val = (weighted[0:1] + lifted_sum) * (1.0 / everyone)
    variance = (weighted[NCELL : NCELL + 1] + jnp.sum(mixed, 0, keepdims=True)) * (
        1.0 / everyone
    ) - mean_val * mean_val
    scale = lax.rsqrt(variance + norm_eps) * gain_ref[...]
    upper, lower = two_parts(projected)
    stack = jnp.concatenate([upper, lower], 0)
    lifted = contract(share_ref[:, :128], stack, ((1,), (0,))) + contract(
        share_ref[:, 128:], stack, ((1,), (0,))
    )
    joined = (direct_ref[...] + lifted - mean_val) * scale + bias_ref[...]
    out_ref[...] = jnp.maximum(joined, 0.0).astype(bf16)


def shards(
    tokens,
    ln_gain,
    ln_bias,
    qkv_weight,
    qkv_bias,
    rel_table,
    proj_weight,
    proj_bias,
    branch_weight,
    branch_bias,
    join_block,
    join_branch,
    bn_gain,
    bn_bias,
):
    row_count, col_count, width = tokens.shape
    nrow, ncol = lax.axis_size("rows"), lax.axis_size("cols")
    height, breadth = row_count * nrow, col_count * ncol
    geo = (row_count, col_count, height, breadth)
    channels = join_block.shape[1]
    count = row_count * col_count
    nwin = count // (WIN * WIN)
    everyone = nrow * ncol
    sizes, starts, total = piece_sizes(row_count, col_count)
    my_row, my_col = lax.axis_index("rows"), lax.axis_index("cols")
    place = jnp.stack([my_row, my_col, my_col % 2]).astype(jnp.int32)

    def shifted(value, down, right):
        pairs = []
        for r in range(nrow):
            for c in range(ncol):
                pairs.append(
                    (r * ncol + c, ((r + down) % nrow) * ncol + (c + right) % ncol)
                )
        return lax.ppermute(value, axes, pairs)

    def exchanged(value, mask):
        return lax.ppermute(value, axes, [(i, i ^ mask) for i in range(everyone)])

    vmem = pl.BlockSpec(memory_space=pltpu.VMEM)
    smem = pl.BlockSpec(memory_space=pltpu.SMEM)

    def flat(piece):
        return piece.reshape(-1, width)

    rr = shifted(flat(tokens[:HALF, HALF:]), -1, 0)
    rd = shifted(flat(tokens[:HALF, :HALF]), -1, -1)
    rc = shifted(flat(tokens[HALF:, :HALF]), 0, -1)
    own = flat(tokens[HALF:, HALF:])
    pair_bias = expanded_bias(rel_table)

    order = np.array(window_order(row_count, col_count), np.float32)
    token_lanes = np.zeros((8, count), np.float32)
    token_lanes[:2] = order.T
    grid = np.zeros((count, 8), np.float32)
    grid[:, 0] = np.arange(count) // col_count
    grid[:, 1] = np.arange(count) % col_count
    cells = cell_table(height, breadth)
    cell_lanes = np.zeros((8, 128), np.float32)
    cell_lanes[:, :64] = cells.T
    cell_lanes[:, 64:] = cells.T
    rows_half = half_rows(width, channels)

    shape = jax.ShapeDtypeStruct
    keep, send, own_b, row_b, col_b, diag_b = pl.pallas_call(
        functools.partial(attention_kernel, geo),
        out_shape=[
            shape((rows_half, 128), f32),
            shape((rows_half, 128), f32),
        ]
        + [shape((size, width), bf16) for size in sizes],
        in_specs=[smem] + [vmem] * 17,
        out_specs=[vmem] * 6,
        scratch_shapes=[
            pltpu.VMEM((total, width), bf16),
            pltpu.VMEM((nwin, WIN * WIN, width), bf16),
            pltpu.VMEM((nwin, WIN * WIN, width), bf16),
            pltpu.VMEM((nwin, width, WIN * WIN), bf16),
            pltpu.VMEM((nwin, width, WIN * WIN), bf16),
            pltpu.VMEM((count, width), bf16),
            pltpu.VMEM((nwin, WIN * WIN, WIN * WIN), f32),
            pltpu.VMEM((2, rows_half, 128), f32),
        ],
        compiler_params=pltpu.CompilerParams(vmem_limit_bytes=40 << 20),
        name="window_attention",
    )(
        place,
        own,
        rr,
        rc,
        rd,
        jnp.asarray(roll_gather(row_count, col_count), bf16),
        jnp.asarray(unroll_scatter(row_count, col_count), bf16),
        ln_gain[None],
        ln_bias[None],
        qkv_weight,
        qkv_bias[None],
        pair_bias,
        proj_weight,
        proj_bias[None],
        join_block,
        jnp.asarray(token_lanes),
        jnp.asarray(cells),
        jnp.asarray(fine_table(height, breadth)),
    )

    rr_b = shifted(row_b, 1, 0)
    rd_b = shifted(diag_b, 1, 1)
    rc_b = shifted(col_b, 0, 1)
    mine = keep + exchanged(send, 1)
    mask = 2
    while mask < everyone:
        mine = mine + exchanged(mine, mask)
        mask *= 2
    other = exchanged(mine, 1)

    direct, share = pl.pallas_call(
        functools.partial(direct_kernel, geo),
        out_shape=[shape((count, channels), f32), shape((count, 256), bf16)],
        in_specs=[smem] + [vmem] * 8,
        out_specs=[vmem] * 2,
        scratch_shapes=[pltpu.VMEM((total, width), bf16)],
        compiler_params=pltpu.CompilerParams(vmem_limit_bytes=16 << 20),
        cost_estimate=pl.CostEstimate(
            flops=2 * count * width * channels, bytes_accessed=4 << 20, transcendentals=0
        ),
        name="direct_join",
    )(
        place,
        own_b,
        rr_b,
        rc_b,
        rd_b,
        jnp.asarray(unroll_gather(row_count, col_count), bf16),
        join_block,
        jnp.asarray(grid),
        jnp.asarray(cell_lanes),
    )

    joined = pl.pallas_call(
        functools.partial(final_kernel, geo),
        out_shape=shape((count, channels), bf16),
        in_specs=[smem] + [vmem] * 11,
        out_specs=vmem,
        scratch_shapes=[
            pltpu.VMEM((2, rows_half, 128), f32),
            pltpu.VMEM((FINE_PAD, width), f32),
            pltpu.VMEM((CELL_PAD, channels), f32),
            pltpu.VMEM((64, channels), f32),
        ],
        compiler_params=pltpu.CompilerParams(vmem_limit_bytes=24 << 20),
        name="final_join",
    )(
        place,
        mine,
        other,
        direct,
        share,
        branch_weight,
        branch_bias,
        join_branch,
        jnp.asarray(group_table()),
        jnp.asarray(gram_tables(height, breadth)),
        bn_gain[None],
        bn_bias[None],
    )
    return joined.reshape(row_count, col_count, channels)


def solution(mesh):
    in_specs = (P("rows", "cols", None),) + (P(),) * 13
    return jax.shard_map(
        shards, mesh=mesh, in_specs=in_specs, out_specs=P("rows", "cols", None), check_vma=False
    )
```

```python
import functools

import jax
import jax.numpy as jnp
import numpy as np
from jax import lax
from jax.experimental import pallas as pl
from jax.experimental.pallas import tpu as pltpu
from jax.sharding import PartitionSpec as P


WIN = 12
HALF = WIN // 2
bin_scales = (1, 2, 3, 6)
norm_eps = 1e-05
highest = lax.Precision.HIGHEST
f32 = jnp.float32
bf16 = jnp.bfloat16
axes = ("rows", "cols")


def up(count, step):
    return -(-count // step) * step


def window_order(row_count, col_count):
    order = []
    for wr in range(row_count // WIN):
        for wc in range(col_count // WIN):
            for p in range(WIN):
                for q in range(WIN):
                    order.append((wr * WIN + p, wc * WIN + q))
    return order


def piece_sizes(row_count, col_count):
    inner_r, inner_c = row_count - HALF, col_count - HALF
    sizes = [inner_r * inner_c, HALF * inner_c, inner_r * HALF, HALF * HALF]
    starts, at = [], 0
    for size in sizes:
        starts.append(at)
        at += up(size, 16)
    return sizes, starts, at


def tile_sizes(row_count, col_count):
    sizes = [row_count * col_count] + piece_sizes(row_count, col_count)[0][1:]
    starts, at = [], 0
    for size in sizes:
        starts.append(at)
        at += up(size, 16)
    return sizes, starts, at


def roll_send(row_count, col_count):
    inner_c = col_count - HALF
    _, starts, total = piece_sizes(row_count, col_count)
    base = starts[1]
    table = np.zeros((total - base, row_count * col_count), np.float32)
    for i in range(row_count):
        for j in range(col_count):
            if i < HALF and j >= HALF:
                target = starts[1] + i * inner_c + (j - HALF)
            elif i < HALF:
                target = starts[3] + i * HALF + j
            elif j < HALF:
                target = starts[2] + (i - HALF) * HALF + j
            else:
                continue
            table[target - base, i * col_count + j] = 1.0
    return table


def roll_gather(row_count, col_count):
    inner_r, inner_c = row_count - HALF, col_count - HALF
    _, starts, total = tile_sizes(row_count, col_count)
    table = np.zeros((row_count * col_count, total), np.float32)
    for token, (i, j) in enumerate(window_order(row_count, col_count)):
        if i < inner_r and j < inner_c:
            source = starts[0] + (i + HALF) * col_count + (j + HALF)
        elif j < inner_c:
            source = starts[1] + (i - inner_r) * inner_c + j
        elif i < inner_r:
            source = starts[2] + i * HALF + (j - inner_c)
        else:
            source = starts[3] + (i - inner_r) * HALF + (j - inner_c)
        table[token, source] = 1.0
    return table


def unroll_scatter(row_count, col_count):
    inner_r, inner_c = row_count - HALF, col_count - HALF
    _, starts, total = piece_sizes(row_count, col_count)
    table = np.zeros((total, row_count * col_count), np.float32)
    for token, (i, j) in enumerate(window_order(row_count, col_count)):
        if i < inner_r and j < inner_c:
            target = starts[0] + i * inner_c + j
        elif j < inner_c:
            target = starts[1] + (i - inner_r) * inner_c + j
        elif i < inner_r:
            target = starts[2] + i * HALF + (j - inner_c)
        else:
            target = starts[3] + (i - inner_r) * HALF + (j - inner_c)
        table[target, token] = 1.0
    return table


def unroll_gather(row_count, col_count):
    inner_c = col_count - HALF
    _, starts, total = piece_sizes(row_count, col_count)
    table = np.zeros((row_count * col_count, total), np.float32)
    for i in range(row_count):
        for j in range(col_count):
            if i >= HALF and j >= HALF:
                source = starts[0] + (i - HALF) * inner_c + (j - HALF)
            elif j >= HALF:
                source = starts[1] + i * inner_c + (j - HALF)
            elif i >= HALF:
                source = starts[2] + (i - HALF) * HALF + j
            else:
                source = starts[3] + i * HALF + j
            table[i * col_count + j, source] = 1.0
    return table


def cell_list():
    cells = []
    for s in bin_scales:
        for a in range(s):
            for b in range(s):
                cells.append((s, a, b))
    return cells


CELLS = cell_list()
NCELL = len(CELLS)
FINE = bin_scales[-1]
NFINE = FINE * FINE
CELL_PAD = up(NCELL + 1, 8)
FINE_PAD = up(NFINE, 8)


def cell_table(height, breadth):
    table = np.zeros((64, 8), np.float32)
    for k, (s, a, b) in enumerate(CELLS):
        table[k, :5] = (s / height, s / breadth, s - 1.0, a, b)
    table[NCELL:, 3] = -9.0
    return table


def fine_table(height, breadth):
    table = np.zeros((FINE_PAD, 8), np.float32)
    table[:, :4] = -1.0
    for a in range(FINE):
        for b in range(FINE):
            table[a * FINE + b, :4] = (
                a * (height // FINE),
                (a + 1) * (height // FINE),
                b * (breadth // FINE),
                (b + 1) * (breadth // FINE),
            )
    return table


def group_table():
    table = np.zeros((64, FINE_PAD), np.float32)
    for k, (s, a, b) in enumerate(CELLS):
        step = FINE // s
        for aa in range(a * step, (a + 1) * step):
            for bb in range(b * step, (b + 1) * step):
                table[k, aa * FINE + bb] = 1.0
    return table


def spread_weights(total, s):
    place = np.clip((np.arange(total) + 0.5) * s / total - 0.5, 0.0, s - 1.0)
    return np.maximum(0.0, 1.0 - np.abs(place[:, None] - np.arange(s)[None, :]))


def gram_tables(height, breadth):
    rows = np.zeros((height, 64))
    cols = np.zeros((breadth, 64))
    for k, (s, a, b) in enumerate(CELLS):
        rows[:, k] = spread_weights(height, s)[:, a]
        cols[:, k] = spread_weights(breadth, s)[:, b]
    gram = (rows.T @ rows) * (cols.T @ cols)
    mass = rows.sum(0) * cols.sum(0)
    gram[NCELL] = mass
    return gram.astype(np.float32)


def send_kernel(geo, tokens_ref, table_ref, rr_ref, rc_ref, rd_ref, tok_ref, tab_ref, sem):
    sizes, starts, _ = piece_sizes(geo[0], geo[1])
    copies = [
        pltpu.make_async_copy(tokens_ref, tok_ref, sem.at[0]),
        pltpu.make_async_copy(table_ref, tab_ref, sem.at[1]),
    ]
    for copy in copies:
        copy.start()
    for copy in copies:
        copy.wait()
    pieces = contract(tab_ref[...], tok_ref[...], ((1,), (0,))).astype(bf16)
    for ref, start, size in zip((rr_ref, rc_ref, rd_ref), starts[1:], sizes[1:]):
        at = start - starts[1]
        ref[...] = pieces[at : at + size]


def bias_kernel(count, table_ref, *refs):
    sources, out_ref = refs[:count], refs[count]
    targets = refs[count + 1 : 2 * count + 1]
    rel_ref, g_ref, sem = refs[2 * count + 1 :]
    copies = [
        pltpu.make_async_copy(source, target, sem.at[k])
        for k, (source, target) in enumerate(zip(sources, targets))
    ]
    for copy in copies:
        copy.start()
    heads = table_ref.shape[2]
    span = 2 * WIN - 1
    for a in range(span):
        rel_ref[:, a, :span] = table_ref[a].T
    lane = lax.broadcasted_iota(jnp.int32, (heads, 16, 128), 2)
    tiles = [jnp.zeros((heads, 16, 128), f32) for _ in range(3)]
    for a in range(span):
        line = rel_ref[:, a : a + 1, :]
        shift = (WIN * a - (WIN - 1)) % 128
        if shift > 112:
            line = pltpu.roll(line, shift, 2)
            shift = 0
        line = jnp.broadcast_to(line, (heads, 16, 128))
        moved = pltpu.roll(line, shift, 2, stride=1, stride_axis=1)
        first, last = WIN * a, WIN * a + WIN
        for t in range(first // 128, (last - 1) // 128 + 1):
            inside = (lane >= first - 128 * t) & (lane < last - 128 * t)
            tiles[t] = jnp.where(inside, moved, tiles[t])
    for t in range(3):
        g_ref[:, :, 128 * t : 128 * t + 128] = tiles[t]
    for u in range(WIN):
        offset = WIN * (WIN - 1 - u)
        wide = g_ref[...]
        if offset:
            wide = pltpu.roll(wide, 384 - offset, 2)
        out_ref[:, WIN * u : WIN * u + WIN, :] = wide[:, :WIN, : WIN * WIN]
    for copy in copies:
        copy.wait()


def expanded_bias(rel_table, *brought):
    heads = rel_table.shape[2]
    tokens = WIN * WIN
    vmem = pl.BlockSpec(memory_space=pltpu.VMEM)
    return pl.pallas_call(
        functools.partial(bias_kernel, len(brought)),
        out_shape=[jax.ShapeDtypeStruct((heads, tokens, tokens), f32)]
        + [jax.ShapeDtypeStruct(x.shape, x.dtype) for x in brought],
        in_specs=[vmem] + [pl.BlockSpec(memory_space=pltpu.HBM)] * len(brought),
        out_specs=[vmem] * (1 + len(brought)),
        scratch_shapes=[
            pltpu.VMEM((heads, 24, 128), f32),
            pltpu.VMEM((heads, 16, 384), f32),
            pltpu.SemaphoreType.DMA((len(brought),)),
        ],
        compiler_params=pltpu.CompilerParams(vmem_limit_bytes=16 << 20),
        cost_estimate=pl.CostEstimate(
            flops=4 * heads * tokens * tokens,
            bytes_accessed=4 * heads * tokens * 256,
            transcendentals=0,
        ),
        name="expand_bias",
    )(rel_table, *[pltpu.with_memory_space_constraint(x, pltpu.HBM) for x in brought])


def contract(a, b, dims, **kw):
    return lax.dot_general(a, b, (dims, ((), ())), preferred_element_type=f32, **kw)


def attention_kernel(
    geo,
    own_ref,
    rr_ref,
    rc_ref,
    rd_ref,
    gather_ref,
    scatter_ref,
    lng_ref,
    lnb_ref,
    wqkv_ref,
    bqkv_ref,
    bias_ref,
    wproj_ref,
    bproj_ref,
    wjoin_ref,
    small_ref,
    keep_ref,
    send_ref,
    o_own_ref,
    o_row_ref,
    o_col_ref,
    o_diag_ref,
    xs_ref,
    q_ref,
    k_ref,
    vt_ref,
    ct_ref,
    blk_ref,
    pen_ref,
    buf_ref,
    sa_ref,
    sb_ref,
    pa_ref,
    pb_ref,
):
    row_count, col_count, height, breadth = geo
    nwr, nwc = row_count // WIN, col_count // WIN
    tokens, width = row_count * col_count, own_ref.shape[1]
    wt = WIN * WIN
    heads = bias_ref.shape[0]
    hd = width // heads
    per_tile = 128 // hd
    my_row, my_col = lax.axis_index("rows"), lax.axis_index("cols")
    bit = lax.rem(my_col, 2)
    sizes, starts, total = tile_sizes(row_count, col_count)
    xs_ref[starts[1] :, :] = jnp.zeros((total - starts[1], width), bf16)
    for ref, start, size in zip((own_ref, rr_ref, rc_ref, rd_ref), starts, sizes):
        xs_ref[start : start + size, :] = ref[...]
    sizes, starts, total = piece_sizes(row_count, col_count)
    rolled = contract(gather_ref[...], xs_ref[...], ((1,), (0,)))
    center = jnp.mean(rolled, -1, keepdims=True)
    delta = rolled - center
    spread = jnp.mean(delta * delta, -1, keepdims=True)
    normed = (delta * lax.rsqrt(spread + norm_eps) * lng_ref[...][None, :] + lnb_ref[...][None, :]).astype(bf16)
    blk_ref[...] = rolled.astype(bf16)
    for part in range(3):
        cols = slice(part * width, (part + 1) * width)
        mixed = contract(normed, wqkv_ref[:, cols], ((1,), (0,))) + bqkv_ref[cols][None, :]
        if part == 0:
            q_ref[...] = (mixed * hd ** (-0.5)).astype(bf16).reshape(q_ref.shape)
        elif part == 1:
            k_ref[...] = mixed.astype(bf16).reshape(k_ref.shape)
        else:
            for w in range(nwr * nwc):
                vt_ref[w] = mixed[w * wt : (w + 1) * wt].T.astype(bf16)

    sub = lax.broadcasted_iota(jnp.int32, (wt, wt), 0)
    lane = lax.broadcasted_iota(jnp.int32, (wt, wt), 1)
    row_diff = (sub < wt // 2) != (lane < wt // 2)
    col_diff = (sub % WIN < HALF) != (lane % WIN < HALF)
    for wr in range(nwr):
        for wc in range(nwc):
            row_last = my_row * nwr + wr == height // WIN - 1
            col_last = my_col * nwc + wc == breadth // WIN - 1
            bad = (row_diff & row_last) | (col_diff & col_last)
            pen_ref[wr * nwc + wc] = jnp.where(bad, -100.0, 0.0)

    head_lane = lax.broadcasted_iota(jnp.int32, (wt, 128), 1) // hd
    tiles = width // 128
    steps = nwr * nwc * tiles

    def make_scores(step, s_ref):
        step = jnp.minimum(step, steps - 1)
        w, at = step // tiles, pl.multiple_of(step % tiles * 128, 128)
        queries = q_ref[w, :, pl.ds(at, 128)]
        keys = k_ref[w, :, pl.ds(at, 128)]
        for hh in range(per_tile):
            keys_h = jnp.where(head_lane == hh, keys, jnp.zeros_like(keys))
            s_ref[hh] = contract(keys_h, queries, ((1,), (1,)))

    def make_weights(step, s_ref, p_ref):
        w, t = step // tiles, step % tiles
        for hh in range(per_tile):
            scores = s_ref[hh] + bias_ref[t * per_tile + hh] + pen_ref[w]
            top = jnp.max(scores, 0, keepdims=True)
            grown = jnp.exp(scores - top)
            scale = 1.0 / jnp.sum(grown, 0, keepdims=True)
            p_ref[hh] = (grown * scale).astype(bf16)

    def make_context(step, p_ref):
        step = jnp.maximum(step, 0)
        w, at = step // tiles, step % tiles * 128
        for hh in range(per_tile):
            place = pl.multiple_of(at + hh * hd, hd)
            context = contract(vt_ref[w, pl.ds(place, hd), :], p_ref[hh], ((1,), (0,)))
            ct_ref[w, pl.ds(place, hd), :] = context.astype(bf16)

    def step_pair(pair, carry):
        step = pair * 2
        make_scores(step + 1, sb_ref)
        make_weights(step, sa_ref, pa_ref)
        make_context(step - 1, pb_ref)
        make_scores(step + 2, sa_ref)
        make_weights(step + 1, sb_ref, pb_ref)
        make_context(step, pa_ref)
        return carry

    make_scores(0, sa_ref)
    lax.fori_loop(0, steps // 2, step_pair, 0)
    make_context(steps - 1, pb_ref)

    for w in range(nwr * nwc):
        attended = contract(ct_ref[w], wproj_ref[...], ((0,), (0,))) + bproj_ref[...][None, :]
        here = slice(w * wt, (w + 1) * wt)
        blk_ref[here, :] = (blk_ref[here, :].astype(f32) + attended).astype(bf16)

    block = blk_ref[...]
    pieces = contract(scatter_ref[...], block, ((1,), (0,))).astype(bf16)
    for ref, start, size in zip((o_own_ref, o_row_ref, o_col_ref, o_diag_ref), starts, sizes):
        ref[...] = pieces[start : start + size]

    row = small_ref[0:1, :tokens] + (my_row * row_count + HALF).astype(f32)
    col = small_ref[1:2, :tokens] + (my_col * col_count + HALF).astype(f32)
    row = jnp.where(row >= height, row - height, row)
    col = jnp.where(col >= breadth, col - breadth, col)
    fine = small_ref[72 : 72 + FINE_PAD, :8]
    inside = (
        (row >= fine[:, 0:1]) & (row < fine[:, 1:2]) & (col >= fine[:, 2:3]) & (col < fine[:, 3:4])
    )
    pooled = contract(inside.astype(bf16), block, ((1,), (0,)))
    cell = small_ref[8 : 8 + CELL_PAD, :8]
    row_at = jnp.clip((row + 0.5) * cell[:, 0:1] - 0.5, 0.0, cell[:, 2:3])
    col_at = jnp.clip((col + 0.5) * cell[:, 1:2] - 0.5, 0.0, cell[:, 2:3])
    share = jnp.maximum(0.0, 1.0 - jnp.abs(row_at - cell[:, 3:4])) * jnp.maximum(
        0.0, 1.0 - jnp.abs(col_at - cell[:, 4:5])
    )
    direct = contract(block, wjoin_ref[...], ((1,), (0,)))
    weighted = contract(share, direct, ((1,), (0,)), precision=highest)
    squares = jnp.sum(direct * direct, 0, keepdims=True)
    which = lax.broadcasted_iota(jnp.int32, weighted.shape, 0)
    weighted = jnp.where(which == NCELL, squares, weighted)
    half_w, half_c = width // 2, direct.shape[1] // 2
    for b in range(2):
        at = 0
        for t in range(half_w // 128):
            lo = b * half_w + t * 128
            buf_ref[b, at : at + FINE_PAD, :] = pooled[:, lo : lo + 128]
            at += FINE_PAD
        for t in range(half_c // 128):
            lo = b * half_c + t * 128
            buf_ref[b, at : at + CELL_PAD, :] = weighted[:, lo : lo + 128]
            at += CELL_PAD
    keep_ref[...] = buf_ref[bit]
    send_ref[...] = buf_ref[1 - bit]


def half_rows(width, channels):
    return FINE_PAD * (width // 256) + CELL_PAD * (channels // 256)


def direct_kernel(
    geo, own_ref, rr_ref, rc_ref, rd_ref, gather_ref, wjoin_ref, token_ref, cell_ref,
    out_ref, share_ref, xs_ref
):
    row_count, col_count, _, _ = geo
    sizes, starts, _ = piece_sizes(row_count, col_count)
    my_row, my_col = lax.axis_index("rows"), lax.axis_index("cols")
    xs_ref[...] = jnp.zeros_like(xs_ref)
    for ref, start, size in zip((own_ref, rr_ref, rc_ref, rd_ref), starts, sizes):
        xs_ref[start : start + size, :] = ref[...]
    block = contract(gather_ref[...], xs_ref[...], ((1,), (0,))).astype(bf16)
    out_ref[...] = contract(block, wjoin_ref[...], ((1,), (0,)))
    row = token_ref[:, 0:1] + (my_row * row_count).astype(f32)
    col = token_ref[:, 1:2] + (my_col * col_count).astype(f32)
    row_at = jnp.clip((row + 0.5) * cell_ref[0:1, :] - 0.5, 0.0, cell_ref[2:3, :])
    col_at = jnp.clip((col + 0.5) * cell_ref[1:2, :] - 0.5, 0.0, cell_ref[2:3, :])
    share = jnp.maximum(0.0, 1.0 - jnp.abs(row_at - cell_ref[3:4, :])) * jnp.maximum(
        0.0, 1.0 - jnp.abs(col_at - cell_ref[4:5, :])
    )
    upper = share.astype(bf16)
    lower = (share - upper.astype(f32)).astype(bf16)
    lane = lax.broadcasted_iota(jnp.int32, share.shape, 1)
    share_ref[:, :128] = upper
    share_ref[:, 128:] = lower


def two_parts(value):
    upper = value.astype(bf16)
    return upper, (value - upper.astype(f32)).astype(bf16)


def final_kernel(
    geo,
    mine_ref,
    other_ref,
    direct_ref,
    share_ref,
    wb_ref,
    bb_ref,
    jb_ref,
    group_ref,
    gram_ref,
    gain_ref,
    bias_ref,
    out_ref,
    buf_ref,
    pool_ref,
    wei_ref,
    proj_ref,
):
    _, _, height, breadth = geo
    bit = lax.rem(lax.axis_index("cols"), 2)
    width, channels = pool_ref.shape[1], wei_ref.shape[1]
    half_w, half_c = width // 2, channels // 2
    buf_ref[bit] = mine_ref[...]
    buf_ref[1 - bit] = other_ref[...]
    for b in range(2):
        at = 0
        for t in range(half_w // 128):
            lo = b * half_w + t * 128
            pool_ref[:, lo : lo + 128] = buf_ref[b, at : at + FINE_PAD, :]
            at += FINE_PAD
        for t in range(half_c // 128):
            lo = b * half_c + t * 128
            wei_ref[:, lo : lo + 128] = buf_ref[b, at : at + CELL_PAD, :]
            at += CELL_PAD
    cells = contract(group_ref[...], pool_ref[...], ((1,), (0,)), precision=highest)
    proj_ref[...] = jnp.zeros_like(proj_ref)
    start = 0
    for k, s in enumerate(bin_scales):
        count = s * s
        scale = 1.0 / float((height // s) * (breadth // s))
        upper, lower = two_parts(cells[start : start + count] * scale)
        hidden = contract(upper, wb_ref[k], ((1,), (0,))) + contract(lower, wb_ref[k], ((1,), (0,)))
        hidden = jnp.maximum(hidden + bb_ref[k : k + 1, :], 0.0)
        upper, lower = two_parts(hidden)
        proj_ref[start : start + count, :] = contract(upper, jb_ref[k], ((1,), (0,))) + contract(
            lower, jb_ref[k], ((1,), (0,))
        )
        start += count
    projected = proj_ref[...]
    everyone = float(height * breadth)
    spun = contract(gram_ref[...], projected, ((1,), (0,)), precision=highest)
    weighted = wei_ref[...]
    lifted_sum = spun[NCELL : NCELL + 1]
    mixed = projected[:NCELL] * (spun[:NCELL] + 2.0 * weighted[:NCELL])
    mean_val = (weighted[0:1] + lifted_sum) * (1.0 / everyone)
    variance = (weighted[NCELL : NCELL + 1] + jnp.sum(mixed, 0, keepdims=True)) * (
        1.0 / everyone
    ) - mean_val * mean_val
    scale = lax.rsqrt(variance + norm_eps) * gain_ref[...][None, :]
    upper, lower = two_parts(projected)
    stack = jnp.concatenate([upper, lower], 0)
    lifted = contract(share_ref[:, :128], stack, ((1,), (0,))) + contract(
        share_ref[:, 128:], stack, ((1,), (0,))
    )
    joined = (direct_ref[...] + lifted - mean_val) * scale + bias_ref[...][None, :]
    out_ref[...] = jnp.maximum(joined, 0.0).astype(bf16)


def shards(
    tokens,
    ln_gain,
    ln_bias,
    qkv_weight,
    qkv_bias,
    rel_table,
    proj_weight,
    proj_bias,
    branch_weight,
    branch_bias,
    join_block,
    join_branch,
    bn_gain,
    bn_bias,
):
    row_count, col_count, width = tokens.shape
    nrow, ncol = lax.axis_size("rows"), lax.axis_size("cols")
    height, breadth = row_count * nrow, col_count * ncol
    geo = (row_count, col_count, height, breadth)
    channels = join_block.shape[1]
    count = row_count * col_count
    nwin = count // (WIN * WIN)
    everyone = nrow * ncol
    sizes, _, total = piece_sizes(row_count, col_count)

    def shifted(value, down, right):
        pairs = []
        for r in range(nrow):
            for c in range(ncol):
                pairs.append(
                    (r * ncol + c, ((r + down) % nrow) * ncol + (c + right) % ncol)
                )
        return lax.ppermute(value, axes, pairs)

    def exchanged(value, mask):
        return lax.ppermute(value, axes, [(i, i ^ mask) for i in range(everyone)])

    vmem = pl.BlockSpec(memory_space=pltpu.VMEM)
    hbm = pl.BlockSpec(memory_space=pltpu.HBM)

    shape = jax.ShapeDtypeStruct
    own = tokens.reshape(count, width)
    send_table = roll_send(row_count, col_count)
    send_rr, send_rc, send_rd = pl.pallas_call(
        functools.partial(send_kernel, geo),
        out_shape=[shape((size, width), bf16) for size in sizes[1:]],
        in_specs=[hbm] * 2,
        out_specs=[vmem] * 3,
        scratch_shapes=[
            pltpu.VMEM((count, width), bf16),
            pltpu.VMEM(send_table.shape, bf16),
            pltpu.SemaphoreType.DMA((2,)),
        ],
        compiler_params=pltpu.CompilerParams(vmem_limit_bytes=8 << 20),
        name="send_pieces",
    )(
        pltpu.with_memory_space_constraint(own, pltpu.HBM),
        pltpu.with_memory_space_constraint(jnp.asarray(send_table, bf16), pltpu.HBM),
    )
    rr = shifted(send_rr, -1, 0)
    rd = shifted(send_rd, -1, -1)
    rc = shifted(send_rc, 0, -1)

    order = np.array(window_order(row_count, col_count), np.float32)
    token_lanes = np.zeros((8, count), np.float32)
    token_lanes[:2] = order.T
    grid = np.zeros((count, 8), np.float32)
    grid[:, 0] = np.arange(count) // col_count
    grid[:, 1] = np.arange(count) % col_count
    cells = cell_table(height, breadth)
    cell_lanes = np.zeros((8, 128), np.float32)
    cell_lanes[:, :64] = cells.T
    cell_lanes[:, 64:] = cells.T
    rows_half = half_rows(width, channels)
    per_tile = 128 // (width // rel_table.shape[2])

    small = np.zeros((128, 384), np.float32)
    small[:8, :count] = token_lanes
    small[8:72, :8] = cells
    small[72 : 72 + FINE_PAD, :8] = fine_table(height, breadth)
    pair_bias, near_proj, near_join, near_gather, near_scatter, near_small, near_own = expanded_bias(
        rel_table,
        proj_weight,
        join_block,
        jnp.asarray(roll_gather(row_count, col_count), bf16),
        jnp.asarray(unroll_scatter(row_count, col_count), bf16),
        jnp.asarray(small),
        own,
    )
    keep, send, own_b, row_b, col_b, diag_b = pl.pallas_call(
        functools.partial(attention_kernel, geo),
        out_shape=[
            shape((rows_half, 128), f32),
            shape((rows_half, 128), f32),
        ]
        + [shape((size, width), bf16) for size in sizes],
        in_specs=[vmem] * 15,
        out_specs=[vmem] * 6,
        scratch_shapes=[
            pltpu.VMEM((tile_sizes(row_count, col_count)[2], width), bf16),
            pltpu.VMEM((nwin, WIN * WIN, width), bf16),
            pltpu.VMEM((nwin, WIN * WIN, width), bf16),
            pltpu.VMEM((nwin, width, WIN * WIN), bf16),
            pltpu.VMEM((nwin, width, WIN * WIN), bf16),
            pltpu.VMEM((count, width), bf16),
            pltpu.VMEM((nwin, WIN * WIN, WIN * WIN), f32),
            pltpu.VMEM((2, rows_half, 128), f32),
            pltpu.VMEM((per_tile, WIN * WIN, WIN * WIN), f32),
            pltpu.VMEM((per_tile, WIN * WIN, WIN * WIN), f32),
            pltpu.VMEM((per_tile, WIN * WIN, WIN * WIN), bf16),
            pltpu.VMEM((per_tile, WIN * WIN, WIN * WIN), bf16),
        ],
        compiler_params=pltpu.CompilerParams(vmem_limit_bytes=24 << 20),
        name="window_attention",
    )(
        near_own,
        rr,
        rc,
        rd,
        near_gather,
        near_scatter,
        ln_gain,
        ln_bias,
        qkv_weight,
        qkv_bias,
        pair_bias,
        near_proj,
        proj_bias,
        near_join,
        near_small,
    )

    rr_b = shifted(row_b, 1, 0)
    rd_b = shifted(diag_b, 1, 1)
    rc_b = shifted(col_b, 0, 1)
    mine = keep + exchanged(send, 1)
    mask = 2
    while mask < everyone:
        mine = mine + exchanged(mine, mask)
        mask *= 2
    other = exchanged(mine, 1)

    direct, share = pl.pallas_call(
        functools.partial(direct_kernel, geo),
        out_shape=[shape((count, channels), f32), shape((count, 256), bf16)],
        in_specs=[vmem] * 8,
        out_specs=[vmem] * 2,
        scratch_shapes=[pltpu.VMEM((total, width), bf16)],
        compiler_params=pltpu.CompilerParams(vmem_limit_bytes=16 << 20),
        cost_estimate=pl.CostEstimate(
            flops=2 * count * width * channels, bytes_accessed=4 << 20, transcendentals=0
        ),
        name="direct_join",
    )(
        own_b,
        rr_b,
        rc_b,
        rd_b,
        jnp.asarray(unroll_gather(row_count, col_count), bf16),
        join_block,
        jnp.asarray(grid),
        jnp.asarray(cell_lanes),
    )

    joined = pl.pallas_call(
        functools.partial(final_kernel, geo),
        out_shape=shape((count, channels), bf16),
        in_specs=[vmem] * 11,
        out_specs=vmem,
        scratch_shapes=[
            pltpu.VMEM((2, rows_half, 128), f32),
            pltpu.VMEM((FINE_PAD, width), f32),
            pltpu.VMEM((CELL_PAD, channels), f32),
            pltpu.VMEM((64, channels), f32),
        ],
        compiler_params=pltpu.CompilerParams(vmem_limit_bytes=24 << 20),
        name="final_join",
    )(
        mine,
        other,
        direct,
        share,
        branch_weight,
        branch_bias,
        join_branch,
        jnp.asarray(group_table()),
        jnp.asarray(gram_tables(height, breadth)),
        bn_gain,
        bn_bias,
    )
    return joined.reshape(row_count, col_count, channels)


def solution(mesh):
    in_specs = (P("rows", "cols", None),) + (P(),) * 13
    return jax.shard_map(
        shards, mesh=mesh, in_specs=in_specs, out_specs=P("rows", "cols", None), check_vma=False
    )
```

```python
import functools

import jax
import jax.numpy as jnp
import numpy as np
from jax import lax
from jax.experimental import pallas as pl
from jax.experimental.pallas import tpu as pltpu
from jax.sharding import PartitionSpec as P


WIN = 12
HALF = WIN // 2
bin_scales = (1, 2, 3, 6)
norm_eps = 1e-05
f32 = jnp.float32
bf16 = jnp.bfloat16
axes = ("rows", "cols")
TAIL = WIN * WIN - 128
GROUP = 128 // TAIL


def up(count, step):
    return -(-count // step) * step


def window_order(row_count, col_count):
    order = []
    for wr in range(row_count // WIN):
        for wc in range(col_count // WIN):
            for p in range(WIN):
                for q in range(WIN):
                    order.append((wr * WIN + p, wc * WIN + q))
    return order


def piece_sizes(row_count, col_count):
    inner_r, inner_c = row_count - HALF, col_count - HALF
    sizes = [inner_r * inner_c, HALF * inner_c, inner_r * HALF, HALF * HALF]
    starts, at = [], 0
    for size in sizes:
        starts.append(at)
        at += up(size, 16)
    return sizes, starts, at


def tile_sizes(row_count, col_count):
    sizes = [row_count * col_count] + piece_sizes(row_count, col_count)[0][1:]
    starts, at = [], 0
    for size in sizes:
        starts.append(at)
        at += up(size, 16)
    return sizes, starts, at


def roll_send(row_count, col_count):
    inner_c = col_count - HALF
    _, starts, total = piece_sizes(row_count, col_count)
    base = starts[1]
    table = np.zeros((total - base, row_count * col_count), np.float32)
    for i in range(row_count):
        for j in range(col_count):
            if i < HALF and j >= HALF:
                target = starts[1] + i * inner_c + (j - HALF)
            elif i < HALF:
                target = starts[3] + i * HALF + j
            elif j < HALF:
                target = starts[2] + (i - HALF) * HALF + j
            else:
                continue
            table[target - base, i * col_count + j] = 1.0
    return table


def roll_gather(row_count, col_count):
    inner_r, inner_c = row_count - HALF, col_count - HALF
    _, starts, total = tile_sizes(row_count, col_count)
    table = np.zeros((row_count * col_count, total), np.float32)
    for token, (i, j) in enumerate(window_order(row_count, col_count)):
        if i < inner_r and j < inner_c:
            source = starts[0] + (i + HALF) * col_count + (j + HALF)
        elif j < inner_c:
            source = starts[1] + (i - inner_r) * inner_c + j
        elif i < inner_r:
            source = starts[2] + i * HALF + (j - inner_c)
        else:
            source = starts[3] + (i - inner_r) * HALF + (j - inner_c)
        table[token, source] = 1.0
    return table


def unroll_scatter(row_count, col_count):
    inner_r, inner_c = row_count - HALF, col_count - HALF
    _, starts, total = piece_sizes(row_count, col_count)
    table = np.zeros((total, row_count * col_count), np.float32)
    for token, (i, j) in enumerate(window_order(row_count, col_count)):
        if i < inner_r and j < inner_c:
            target = starts[0] + i * inner_c + j
        elif j < inner_c:
            target = starts[1] + (i - inner_r) * inner_c + j
        elif i < inner_r:
            target = starts[2] + i * HALF + (j - inner_c)
        else:
            target = starts[3] + (i - inner_r) * HALF + (j - inner_c)
        table[target, token] = 1.0
    return table


def unroll_gather(row_count, col_count):
    inner_c = col_count - HALF
    _, starts, total = piece_sizes(row_count, col_count)
    table = np.zeros((row_count * col_count, total), np.float32)
    for i in range(row_count):
        for j in range(col_count):
            if i >= HALF and j >= HALF:
                source = starts[0] + (i - HALF) * inner_c + (j - HALF)
            elif j >= HALF:
                source = starts[1] + i * inner_c + (j - HALF)
            elif i >= HALF:
                source = starts[2] + (i - HALF) * HALF + j
            else:
                source = starts[3] + i * HALF + j
            table[i * col_count + j, source] = 1.0
    return table


def cell_list():
    cells = []
    for s in bin_scales:
        for a in range(s):
            for b in range(s):
                cells.append((s, a, b))
    return cells


CELLS = cell_list()
NCELL = len(CELLS)
FINE = bin_scales[-1]
NFINE = FINE * FINE
FINE_PAD = up(NFINE, 8)
SENT = [k for k, (s, _, _) in enumerate(CELLS) if s == FINE or (s > 1 and (FINE // s) % 2 == 0)]
NSENT = len(SENT)
CELL_PAD = up(NSENT + 1, 8)


def cell_table(height, breadth, sent):
    chosen = [CELLS[k] for k in SENT] if sent else CELLS
    table = np.zeros((64, 8), np.float32)
    for k, (s, a, b) in enumerate(chosen):
        table[k, :5] = (s / height, s / breadth, s - 1.0, a, b)
    table[len(chosen) :, 3] = -9.0
    return table


def spread_table():
    table = np.zeros((64, CELL_PAD), np.float32)
    for k, (s, a, b) in enumerate(CELLS):
        if k in SENT:
            table[k, SENT.index(k)] = 1.0
            continue
        for m, sent in enumerate(SENT):
            t, aa, bb = CELLS[sent]
            if t == FINE:
                row = np.clip((aa + 0.5) * s / FINE - 0.5, 0.0, s - 1.0)
                col = np.clip((bb + 0.5) * s / FINE - 0.5, 0.0, s - 1.0)
                table[k, m] = max(0.0, 1.0 - abs(row - a)) * max(0.0, 1.0 - abs(col - b))
    return table


def fine_table(height, breadth):
    table = np.zeros((FINE_PAD, 8), np.float32)
    table[:, :4] = -1.0
    for a in range(FINE):
        for b in range(FINE):
            table[a * FINE + b, :4] = (
                a * (height // FINE),
                (a + 1) * (height // FINE),
                b * (breadth // FINE),
                (b + 1) * (breadth // FINE),
            )
    return table


def cell_slots():
    slots, at = [], 0
    for s in bin_scales:
        slots.append((at, up(s * s, 8)))
        at += up(s * s, 8)
    return slots, at


def group_table():
    slots, total = cell_slots()
    table = np.zeros((total, FINE_PAD), np.float32)
    for (first, _), s in zip(slots, bin_scales):
        step = FINE // s
        for a in range(s):
            for b in range(s):
                for aa in range(a * step, (a + 1) * step):
                    for bb in range(b * step, (b + 1) * step):
                        table[first + a * s + b, aa * FINE + bb] = 1.0
    return np.concatenate([table] * 3, 1)


def spread_weights(total, s):
    place = np.clip((np.arange(total) + 0.5) * s / total - 0.5, 0.0, s - 1.0)
    return np.maximum(0.0, 1.0 - np.abs(place[:, None] - np.arange(s)[None, :]))


def gram_tables(height, breadth):
    rows = np.zeros((height, 64))
    cols = np.zeros((breadth, 64))
    for k, (s, a, b) in enumerate(CELLS):
        rows[:, k] = spread_weights(height, s)[:, a]
        cols[:, k] = spread_weights(breadth, s)[:, b]
    gram = (rows.T @ rows) * (cols.T @ cols)
    mass = rows.sum(0) * cols.sum(0)
    gram[NCELL] = mass
    both = np.zeros((up(64 + CELL_PAD, 16), 64))
    both[:64] = gram
    both[64 : 64 + NSENT] = spread_table().T[:NSENT]
    parts = []
    for _ in range(3):
        part = both.astype(jnp.bfloat16).astype(np.float64)
        parts.append(part)
        both = both - part
    table = np.concatenate(parts, 0)
    return np.concatenate([table] * 3, 1).astype(np.float32)


def send_kernel(
    geo, tokens_ref, table_ref, rel_ref, rr_ref, rc_ref, rd_ref, rel_out_ref, tok_ref, tab_ref, sem
):
    sizes, starts, _ = piece_sizes(geo[0], geo[1])
    copies = [
        pltpu.make_async_copy(tokens_ref, tok_ref, sem.at[0]),
        pltpu.make_async_copy(table_ref, tab_ref, sem.at[1]),
        pltpu.make_async_copy(rel_ref, rel_out_ref, sem.at[2]),
    ]
    for copy in copies:
        copy.start()
    for copy in copies:
        copy.wait()
    pieces = contract(tab_ref[...], tok_ref[...], ((1,), (0,))).astype(bf16)
    for ref, start, size in zip((rr_ref, rc_ref, rd_ref), starts[1:], sizes[1:]):
        at = start - starts[1]
        ref[...] = pieces[at : at + size]


def bias_kernel(count, table_ref, *refs):
    sources, out_ref = refs[:count], refs[count]
    targets = refs[count + 1 : 2 * count + 1]
    line_ref, sem = refs[2 * count + 1 :]
    copies = [
        pltpu.make_async_copy(source, target, sem.at[k])
        for k, (source, target) in enumerate(zip(sources, targets))
    ]
    for copy in copies:
        copy.start()
    heads = table_ref.shape[2]
    span = 2 * WIN - 1
    line_ref[...] = jnp.zeros_like(line_ref)
    for a in range(span):
        line_ref[a % 2, :, WIN * a : WIN * a + span] = table_ref[a].T
    wide = [
        [
            jnp.broadcast_to(line_ref[par, :, 128 * t : 128 * t + 128][:, None, :], (heads, 8, 128))
            for t in range(3)
        ]
        for par in range(2)
    ]
    lane = lax.broadcasted_iota(jnp.int32, (8, 128), 1)
    sub = lax.broadcasted_iota(jnp.int32, (8, 128), 0)
    tail = WIN * WIN - 128
    per_slot = 128 // tail
    for k in range(WIN * WIN // 8):
        base = WIN * WIN - 8 - 8 * k
        tile, rest = base // 128, base % 128
        moved = []
        for par in range(2):
            rolled = [
                pltpu.roll(wide[par][t], 121 - rest, 2, stride=1, stride_axis=1)
                for t in range(tile, min(tile + 3, 3))
            ]
            near = lane < 121 - rest + sub
            first = jnp.where(near[None], rolled[0], rolled[1])
            second = rolled[1]
            if rest + 7 + tail > 128:
                second = jnp.where(near[None], rolled[1], rolled[2])
            moved.append((first, second))
        u = (8 * k + sub) // WIN
        rows = slice(8 * k, 8 * k + 8)
        for half in range(2):
            odd = ((128 * half + lane) // WIN + u) % 2 == 1
            result = jnp.where(odd[None], moved[0][half], moved[1][half])
            for g in range(heads // per_slot):
                part = result[g * per_slot : (g + 1) * per_slot]
                slot = g * (per_slot + 1)
                if half == 0:
                    out_ref[slot : slot + per_slot, rows, :] = part
                    continue
                part = jnp.where((lane < tail)[None], part, 0.0)
                pieces = [part[0]] + [
                    pltpu.roll(part[h], tail * h, 1) for h in range(1, per_slot)
                ]
                while len(pieces) > 1:
                    pieces = [x + y for x, y in zip(pieces[::2], pieces[1::2])]
                out_ref[slot + per_slot, rows, :] = pieces[0]
    for copy in copies:
        copy.wait()


def expanded_bias(rel_table, *brought):
    heads = rel_table.shape[2]
    tokens = WIN * WIN
    vmem = pl.BlockSpec(memory_space=pltpu.VMEM)
    return pl.pallas_call(
        functools.partial(bias_kernel, len(brought)),
        out_shape=[jax.ShapeDtypeStruct((heads // GROUP * (GROUP + 1), tokens, 128), f32)]
        + [jax.ShapeDtypeStruct(x.shape, x.dtype) for x in brought],
        in_specs=[vmem] + [pl.BlockSpec(memory_space=pltpu.HBM)] * len(brought),
        out_specs=[vmem] * (1 + len(brought)),
        scratch_shapes=[
            pltpu.VMEM((2, heads, 384), f32),
            pltpu.SemaphoreType.DMA((len(brought),)),
        ],
        compiler_params=pltpu.CompilerParams(vmem_limit_bytes=16 << 20),
        cost_estimate=pl.CostEstimate(
            flops=4 * heads * tokens * tokens,
            bytes_accessed=4 * heads * tokens * 144,
            transcendentals=0,
        ),
        name="expand_bias",
    )(rel_table, *[pltpu.with_memory_space_constraint(x, pltpu.HBM) for x in brought])


def contract(a, b, dims, **kw):
    return lax.dot_general(a, b, (dims, ((), ())), preferred_element_type=f32, **kw)


def f32_parts(value):
    first = value.astype(bf16).astype(f32)
    rest = value - first
    second = rest.astype(bf16).astype(f32)
    return [first, second, (rest - second).astype(bf16).astype(f32)]


def folded(value):
    count = value.shape[0] // 3
    return value[:count] + (value[count : 2 * count] + value[2 * count :])


def attention_kernel(
    geo,
    own_ref,
    rr_ref,
    rc_ref,
    rd_ref,
    gather_ref,
    scatter_ref,
    lng_ref,
    lnb_ref,
    wqkv_ref,
    bqkv_ref,
    bias_ref,
    wproj_ref,
    bproj_ref,
    wjoin_ref,
    small_ref,
    keep_ref,
    send_ref,
    o_own_ref,
    o_row_ref,
    o_col_ref,
    o_diag_ref,
    xs_ref,
    q_ref,
    k_ref,
    vt_ref,
    ct_ref,
    blk_ref,
    pen_ref,
    buf_ref,
    sa_ref,
    sb_ref,
    pa_ref,
    pb_ref,
):
    row_count, col_count, height, breadth = geo
    nwr, nwc = row_count // WIN, col_count // WIN
    tokens, width = row_count * col_count, own_ref.shape[1]
    wt = WIN * WIN
    heads = bias_ref.shape[0] // (GROUP + 1) * GROUP
    hd = width // heads
    per_tile = 128 // hd
    my_row, my_col = lax.axis_index("rows"), lax.axis_index("cols")
    bit = lax.rem(my_col, 2)
    sizes, starts, total = tile_sizes(row_count, col_count)
    xs_ref[starts[1] :, :] = jnp.zeros((total - starts[1], width), bf16)
    for ref, start, size in zip((own_ref, rr_ref, rc_ref, rd_ref), starts, sizes):
        xs_ref[start : start + size, :] = ref[...]
    sizes, starts, total = piece_sizes(row_count, col_count)
    rolled = contract(gather_ref[...], xs_ref[...], ((1,), (0,)))
    center = jnp.mean(rolled, -1, keepdims=True)
    delta = rolled - center
    spread = jnp.mean(delta * delta, -1, keepdims=True)
    normed = (delta * lax.rsqrt(spread + norm_eps) * lng_ref[...][None, :] + lnb_ref[...][None, :]).astype(bf16)
    blk_ref[...] = rolled.astype(bf16)
    for part in range(3):
        cols = slice(part * width, (part + 1) * width)
        mixed = contract(normed, wqkv_ref[:, cols], ((1,), (0,))) + bqkv_ref[cols][None, :]
        if part == 0:
            q_ref[...] = (mixed * hd ** (-0.5)).astype(bf16).reshape(q_ref.shape)
        elif part == 1:
            k_ref[...] = mixed.astype(bf16).reshape(k_ref.shape)
        else:
            for w in range(nwr * nwc):
                vt_ref[w] = mixed[w * wt : (w + 1) * wt].T.astype(bf16)

    sub = lax.broadcasted_iota(jnp.int32, (wt, 128), 0)
    lane = lax.broadcasted_iota(jnp.int32, (wt, 128), 1)
    for kind, query in enumerate((lane, 128 + lane % TAIL)):
        row_diff = (sub < wt // 2) != (query < wt // 2)
        col_diff = (sub % WIN < HALF) != (query % WIN < HALF)
        for wr in range(nwr):
            for wc in range(nwc):
                row_last = my_row * nwr + wr == height // WIN - 1
                col_last = my_col * nwc + wc == breadth // WIN - 1
                bad = (row_diff & row_last) | (col_diff & col_last)
                pen_ref[kind, wr * nwc + wc] = jnp.where(bad, -100.0, 0.0)

    head_lane = lax.broadcasted_iota(jnp.int32, (wt, 128), 1) // hd
    span = GROUP * hd
    joint_shape = (GROUP * TAIL, span)
    joint_own = (
        lax.broadcasted_iota(jnp.int32, joint_shape, 0) // TAIL
        == lax.broadcasted_iota(jnp.int32, joint_shape, 1) // hd
    )
    groups = heads // GROUP
    steps = nwr * nwc * groups

    def make_scores(step, s_ref):
        step = jnp.minimum(step, steps - 1)
        w, g = step // groups, step % groups
        for h in range(GROUP):
            at = pl.multiple_of(g * span + h // per_tile * 128, 128)
            keys = k_ref[w, :, pl.ds(at, 128)]
            keys = jnp.where(head_lane == h % per_tile, keys, jnp.zeros_like(keys))
            s_ref[h] = contract(keys, q_ref[w, :128, pl.ds(at, 128)], ((1,), (1,)))
        at = pl.multiple_of(g * span, span)
        joint = jnp.concatenate([q_ref[w, 128:, pl.ds(at, span)]] * GROUP, 0)
        joint = jnp.where(joint_own, joint, jnp.zeros_like(joint))
        s_ref[GROUP] = contract(k_ref[w, :, pl.ds(at, span)], joint, ((1,), (1,)))

    def make_weights(step, s_ref, p_ref):
        w, g = step // groups, step % groups
        for h in range(GROUP + 1):
            scores = s_ref[h] + bias_ref[g * (GROUP + 1) + h] + pen_ref[h // GROUP, w]
            top = jnp.max(scores, 0, keepdims=True)
            grown = jnp.exp(scores - top)
            scale = 1.0 / jnp.sum(grown, 0, keepdims=True)
            p_ref[h] = (grown * scale).astype(bf16)

    def make_context(step, p_ref):
        step = jnp.maximum(step, 0)
        w, g = step // groups, step % groups
        first = pl.multiple_of(g * span, span)
        joint = contract(vt_ref[w, pl.ds(first, span), :], p_ref[GROUP], ((1,), (0,)))
        for h in range(GROUP):
            place = pl.multiple_of(first + h * hd, hd)
            context = contract(vt_ref[w, pl.ds(place, hd), :], p_ref[h], ((1,), (0,)))
            ct_ref[w, pl.ds(place, hd), :128] = context.astype(bf16)
            rest = joint[h * hd : (h + 1) * hd]
            if h:
                rest = pltpu.roll(rest, 128 - TAIL * h, 1)
            ct_ref[w, pl.ds(place, hd), 128:] = rest[:, :TAIL].astype(bf16)

    def step_pair(pair, carry):
        step = pair * 2
        make_scores(step + 1, sb_ref)
        make_weights(step, sa_ref, pa_ref)
        make_context(step - 1, pb_ref)
        make_scores(step + 2, sa_ref)
        make_weights(step + 1, sb_ref, pb_ref)
        make_context(step, pa_ref)
        return carry

    make_scores(0, sa_ref)
    lax.fori_loop(0, steps // 2, step_pair, 0)
    make_context(steps - 1, pb_ref)

    for w in range(nwr * nwc):
        attended = contract(ct_ref[w], wproj_ref[...], ((0,), (0,))) + bproj_ref[...][None, :]
        here = slice(w * wt, (w + 1) * wt)
        blk_ref[here, :] = (blk_ref[here, :].astype(f32) + attended).astype(bf16)

    block = blk_ref[...]
    pieces = contract(scatter_ref[...], block, ((1,), (0,))).astype(bf16)
    for ref, start, size in zip((o_own_ref, o_row_ref, o_col_ref, o_diag_ref), starts, sizes):
        ref[...] = pieces[start : start + size]

    row = small_ref[0:1, :tokens] + (my_row * row_count + HALF).astype(f32)
    col = small_ref[1:2, :tokens] + (my_col * col_count + HALF).astype(f32)
    row = jnp.where(row >= height, row - height, row)
    col = jnp.where(col >= breadth, col - breadth, col)
    fine = small_ref[72 : 72 + FINE_PAD, :8]
    inside = (
        (row >= fine[:, 0:1]) & (row < fine[:, 1:2]) & (col >= fine[:, 2:3]) & (col < fine[:, 3:4])
    )
    cell = small_ref[8 : 8 + CELL_PAD, :8]
    row_at = jnp.clip((row + 0.5) * cell[:, 0:1] - 0.5, 0.0, cell[:, 2:3])
    col_at = jnp.clip((col + 0.5) * cell[:, 1:2] - 0.5, 0.0, cell[:, 2:3])
    share = jnp.maximum(0.0, 1.0 - jnp.abs(row_at - cell[:, 3:4])) * jnp.maximum(
        0.0, 1.0 - jnp.abs(col_at - cell[:, 4:5])
    )
    picks = jnp.concatenate([inside.astype(f32), *f32_parts(share)], 0).astype(bf16)
    picked = contract(picks, block, ((1,), (0,)))
    pooled = picked[:FINE_PAD]
    lifted = folded(picked[FINE_PAD:])
    both = jnp.concatenate([block, jnp.concatenate(f32_parts(lifted), 0).astype(bf16)], 0)
    joined = contract(both, wjoin_ref[...], ((1,), (0,)))
    direct, weighted = joined[:tokens], folded(joined[tokens:])
    squares = jnp.sum(direct * direct, 0, keepdims=True)
    which = lax.broadcasted_iota(jnp.int32, weighted.shape, 0)
    weighted = jnp.where(which == NSENT, squares, weighted)
    half_w, half_c = width // 2, direct.shape[1] // 2
    for b in range(2):
        at = 0
        for t in range(half_w // 128):
            lo = b * half_w + t * 128
            buf_ref[b, at : at + NFINE, :] = pooled[:NFINE, lo : lo + 128]
            at += NFINE
        for t in range(half_c // 128):
            lo = b * half_c + t * 128
            buf_ref[b, at : at + NSENT + 1, :] = weighted[: NSENT + 1, lo : lo + 128]
            at += NSENT + 1
        if at < buf_ref.shape[1]:
            buf_ref[b, at:, :] = jnp.zeros((buf_ref.shape[1] - at, 128), f32)
    keep_ref[...] = buf_ref[bit]
    send_ref[...] = buf_ref[1 - bit]


def half_rows(width, channels):
    return up(NFINE * (width // 256) + (NSENT + 1) * (channels // 256), 8)


def direct_kernel(
    geo, own_ref, rr_ref, rc_ref, rd_ref, gather_ref, wjoin_ref, token_ref, cell_ref,
    out_ref, share_ref, xs_ref
):
    row_count, col_count, _, _ = geo
    sizes, starts, _ = piece_sizes(row_count, col_count)
    my_row, my_col = lax.axis_index("rows"), lax.axis_index("cols")
    xs_ref[...] = jnp.zeros_like(xs_ref)
    for ref, start, size in zip((own_ref, rr_ref, rc_ref, rd_ref), starts, sizes):
        xs_ref[start : start + size, :] = ref[...]
    block = contract(gather_ref[...], xs_ref[...], ((1,), (0,))).astype(bf16)
    out_ref[...] = contract(block, wjoin_ref[...], ((1,), (0,)))
    row = token_ref[:, 0:1] + (my_row * row_count).astype(f32)
    col = token_ref[:, 1:2] + (my_col * col_count).astype(f32)
    row_at = jnp.clip((row + 0.5) * cell_ref[0:1, :] - 0.5, 0.0, cell_ref[2:3, :])
    col_at = jnp.clip((col + 0.5) * cell_ref[1:2, :] - 0.5, 0.0, cell_ref[2:3, :])
    share = jnp.maximum(0.0, 1.0 - jnp.abs(row_at - cell_ref[3:4, :])) * jnp.maximum(
        0.0, 1.0 - jnp.abs(col_at - cell_ref[4:5, :])
    )
    upper = share.astype(bf16)
    lower = (share - upper.astype(f32)).astype(bf16)
    share_ref[:, :128] = upper
    share_ref[:, 128:] = lower


def two_part_dot(value, weight):
    first = value.astype(bf16).astype(f32)
    parts = jnp.concatenate([first, value - first], 0).astype(bf16)
    product = contract(parts, weight, ((1,), (0,)))
    return product[: value.shape[0]] + product[value.shape[0] :]


def final_kernel(
    geo,
    mine_ref,
    other_ref,
    direct_ref,
    share_ref,
    wb_ref,
    bb_ref,
    jb_ref,
    group_ref,
    gram_ref,
    gain_ref,
    bias_ref,
    out_ref,
    buf_ref,
    pool_ref,
    wei_ref,
    proj_ref,
):
    _, _, height, breadth = geo
    bit = lax.rem(lax.axis_index("cols"), 2)
    width, channels = pool_ref.shape[1], wei_ref.shape[1]
    half_w, half_c = width // 2, channels // 2
    buf_ref[bit] = mine_ref[...]
    buf_ref[1 - bit] = other_ref[...]
    pool_ref[NFINE:, :] = jnp.zeros((pool_ref.shape[0] - NFINE, width), f32)
    wei_ref[NSENT + 1 :, :] = jnp.zeros((wei_ref.shape[0] - NSENT - 1, channels), f32)
    for b in range(2):
        at = 0
        for t in range(half_w // 128):
            lo = b * half_w + t * 128
            pool_ref[:NFINE, lo : lo + 128] = buf_ref[b, at : at + NFINE, :]
            at += NFINE
        for t in range(half_c // 128):
            lo = b * half_c + t * 128
            wei_ref[: NSENT + 1, lo : lo + 128] = buf_ref[b, at : at + NSENT + 1, :]
            at += NSENT + 1
    pool = jnp.concatenate(f32_parts(pool_ref[...]), 0).astype(bf16)
    cells = contract(group_ref[...], pool, ((1,), (0,)))
    proj_ref[...] = jnp.zeros_like(proj_ref)
    start = 0
    for k, (s, (first, count)) in enumerate(zip(bin_scales, cell_slots()[0])):
        scale = 1.0 / float((height // s) * (breadth // s))
        hidden = two_part_dot(cells[first : first + count] * scale, wb_ref[k])
        hidden = jnp.maximum(hidden + bb_ref[k : k + 1, :], 0.0)
        lift = two_part_dot(hidden, jb_ref[k])
        proj_ref[start : start + s * s, :] = lift[: s * s]
        start += s * s
    projected = proj_ref[...]
    parts = [part.astype(bf16) for part in f32_parts(projected)]
    everyone = float(height * breadth)
    spun = folded(contract(gram_ref[...], jnp.concatenate(parts, 0), ((1,), (0,))))
    weighted = wei_ref[...]
    which = lax.broadcasted_iota(jnp.int32, weighted.shape, 0)
    finest = jnp.where((which >= NSENT - NFINE) & (which < NSENT), weighted, 0.0)
    mean_val = (jnp.sum(finest, 0, keepdims=True) + spun[NCELL : NCELL + 1]) * (1.0 / everyone)
    cross = jnp.sum(weighted * spun[64 : 64 + CELL_PAD], 0, keepdims=True)
    square = jnp.sum(projected * spun[:64], 0, keepdims=True)
    variance = (weighted[NSENT : NSENT + 1] + 2.0 * cross + square) * (
        1.0 / everyone
    ) - mean_val * mean_val
    scale = lax.rsqrt(variance + norm_eps) * gain_ref[...][None, :]
    stack = jnp.concatenate(parts[:2] * 2, 0)
    lifted = contract(share_ref[...], stack, ((1,), (0,)))
    joined = (direct_ref[...] + lifted - mean_val) * scale + bias_ref[...][None, :]
    out_ref[...] = jnp.maximum(joined, 0.0).astype(bf16)


def shards(
    tokens,
    ln_gain,
    ln_bias,
    qkv_weight,
    qkv_bias,
    rel_table,
    proj_weight,
    proj_bias,
    branch_weight,
    branch_bias,
    join_block,
    join_branch,
    bn_gain,
    bn_bias,
):
    row_count, col_count, width = tokens.shape
    nrow, ncol = lax.axis_size("rows"), lax.axis_size("cols")
    height, breadth = row_count * nrow, col_count * ncol
    geo = (row_count, col_count, height, breadth)
    channels = join_block.shape[1]
    count = row_count * col_count
    nwin = count // (WIN * WIN)
    everyone = nrow * ncol
    sizes, _, total = piece_sizes(row_count, col_count)

    def shifted(value, down, right):
        pairs = []
        for r in range(nrow):
            for c in range(ncol):
                pairs.append(
                    (r * ncol + c, ((r + down) % nrow) * ncol + (c + right) % ncol)
                )
        return lax.ppermute(value, axes, pairs)

    def exchanged(value, mask):
        return lax.ppermute(value, axes, [(i, i ^ mask) for i in range(everyone)])

    vmem = pl.BlockSpec(memory_space=pltpu.VMEM)
    hbm = pl.BlockSpec(memory_space=pltpu.HBM)

    shape = jax.ShapeDtypeStruct
    own = tokens.reshape(count, width)
    send_table = roll_send(row_count, col_count)
    send_rr, send_rc, send_rd, near_rel = pl.pallas_call(
        functools.partial(send_kernel, geo),
        out_shape=[shape((size, width), bf16) for size in sizes[1:]]
        + [shape(rel_table.shape, rel_table.dtype)],
        in_specs=[hbm] * 3,
        out_specs=[vmem] * 4,
        scratch_shapes=[
            pltpu.VMEM((count, width), bf16),
            pltpu.VMEM(send_table.shape, bf16),
            pltpu.SemaphoreType.DMA((3,)),
        ],
        compiler_params=pltpu.CompilerParams(vmem_limit_bytes=8 << 20),
        name="send_pieces",
    )(
        pltpu.with_memory_space_constraint(own, pltpu.HBM),
        pltpu.with_memory_space_constraint(jnp.asarray(send_table, bf16), pltpu.HBM),
        pltpu.with_memory_space_constraint(rel_table, pltpu.HBM),
    )
    rr = shifted(send_rr, -1, 0)
    rd = shifted(send_rd, -1, -1)
    rc = shifted(send_rc, 0, -1)

    order = np.array(window_order(row_count, col_count), np.float32)
    token_lanes = np.zeros((8, count), np.float32)
    token_lanes[:2] = order.T
    grid = np.zeros((count, 8), np.float32)
    grid[:, 0] = np.arange(count) // col_count
    grid[:, 1] = np.arange(count) % col_count
    cells = cell_table(height, breadth, False)
    sent_cells = cell_table(height, breadth, True)
    cell_lanes = np.zeros((8, 128), np.float32)
    cell_lanes[:, :64] = cells.T
    cell_lanes[:, 64:] = cells.T
    rows_half = half_rows(width, channels)

    small = np.zeros((128, 384), np.float32)
    small[:8, :count] = token_lanes
    small[8:72, :8] = sent_cells
    small[72 : 72 + FINE_PAD, :8] = fine_table(height, breadth)
    pair_bias, near_proj, near_join, near_gather, near_scatter, near_small, near_own = expanded_bias(
        near_rel,
        proj_weight,
        join_block,
        jnp.asarray(roll_gather(row_count, col_count), bf16),
        jnp.asarray(unroll_scatter(row_count, col_count), bf16),
        jnp.asarray(small),
        own,
    )
    keep, send, own_b, row_b, col_b, diag_b = pl.pallas_call(
        functools.partial(attention_kernel, geo),
        out_shape=[
            shape((rows_half, 128), f32),
            shape((rows_half, 128), f32),
        ]
        + [shape((size, width), bf16) for size in sizes],
        in_specs=[vmem] * 15,
        out_specs=[vmem] * 6,
        scratch_shapes=[
            pltpu.VMEM((tile_sizes(row_count, col_count)[2], width), bf16),
            pltpu.VMEM((nwin, WIN * WIN, width), bf16),
            pltpu.VMEM((nwin, WIN * WIN, width), bf16),
            pltpu.VMEM((nwin, width, WIN * WIN), bf16),
            pltpu.VMEM((nwin, width, WIN * WIN), bf16),
            pltpu.VMEM((count, width), bf16),
            pltpu.VMEM((2, nwin, WIN * WIN, 128), f32),
            pltpu.VMEM((2, rows_half, 128), f32),
            pltpu.VMEM((GROUP + 1, WIN * WIN, 128), f32),
            pltpu.VMEM((GROUP + 1, WIN * WIN, 128), f32),
            pltpu.VMEM((GROUP + 1, WIN * WIN, 128), bf16),
            pltpu.VMEM((GROUP + 1, WIN * WIN, 128), bf16),
        ],
        compiler_params=pltpu.CompilerParams(vmem_limit_bytes=24 << 20),
        name="window_attention",
    )(
        near_own,
        rr,
        rc,
        rd,
        near_gather,
        near_scatter,
        ln_gain,
        ln_bias,
        qkv_weight,
        qkv_bias,
        pair_bias,
        near_proj,
        proj_bias,
        near_join,
        near_small,
    )

    rr_b = shifted(row_b, 1, 0)
    rd_b = shifted(diag_b, 1, 1)
    rc_b = shifted(col_b, 0, 1)
    mine = keep + exchanged(send, 1)
    mask = 2
    while mask < everyone:
        mine = mine + exchanged(mine, mask)
        mask *= 2
    other = exchanged(mine, 1)

    direct, share = pl.pallas_call(
        functools.partial(direct_kernel, geo),
        out_shape=[shape((count, channels), f32), shape((count, 256), bf16)],
        in_specs=[vmem] * 8,
        out_specs=[vmem] * 2,
        scratch_shapes=[pltpu.VMEM((total, width), bf16)],
        compiler_params=pltpu.CompilerParams(vmem_limit_bytes=16 << 20),
        cost_estimate=pl.CostEstimate(
            flops=2 * count * width * channels, bytes_accessed=4 << 20, transcendentals=0
        ),
        name="direct_join",
    )(
        own_b,
        rr_b,
        rc_b,
        rd_b,
        jnp.asarray(unroll_gather(row_count, col_count), bf16),
        join_block,
        jnp.asarray(grid),
        jnp.asarray(cell_lanes),
    )

    joined = pl.pallas_call(
        functools.partial(final_kernel, geo),
        out_shape=shape((count, channels), bf16),
        in_specs=[vmem] * 11,
        out_specs=vmem,
        scratch_shapes=[
            pltpu.VMEM((2, rows_half, 128), f32),
            pltpu.VMEM((FINE_PAD, width), f32),
            pltpu.VMEM((CELL_PAD, channels), f32),
            pltpu.VMEM((64, channels), f32),
        ],
        compiler_params=pltpu.CompilerParams(vmem_limit_bytes=24 << 20),
        name="final_join",
    )(
        mine,
        other,
        direct,
        share,
        branch_weight,
        branch_bias,
        join_branch,
        jnp.asarray(group_table(), bf16),
        jnp.asarray(gram_tables(height, breadth), bf16),
        bn_gain,
        bn_bias,
    )
    return joined.reshape(row_count, col_count, channels)


def solution(mesh):
    in_specs = (P("rows", "cols", None),) + (P(),) * 13
    return jax.shard_map(
        shards, mesh=mesh, in_specs=in_specs, out_specs=P("rows", "cols", None), check_vma=False
    )
```

```python
import functools

import jax
import jax.numpy as jnp
import numpy as np
from jax import lax
from jax.experimental import pallas as pl
from jax.experimental.pallas import tpu as pltpu
from jax.sharding import PartitionSpec as P


WIN = 12
HALF = WIN // 2
bin_scales = (1, 2, 3, 6)
norm_eps = 1e-05
f32 = jnp.float32
bf16 = jnp.bfloat16
axes = ("rows", "cols")
TAIL = WIN * WIN - 128
GROUP = 128 // TAIL


def up(count, step):
    return -(-count // step) * step


def window_order(row_count, col_count):
    order = []
    for wr in range(row_count // WIN):
        for wc in range(col_count // WIN):
            for p in range(WIN):
                for q in range(WIN):
                    order.append((wr * WIN + p, wc * WIN + q))
    return order


def piece_sizes(row_count, col_count):
    inner_r, inner_c = row_count - HALF, col_count - HALF
    sizes = [inner_r * inner_c, HALF * inner_c, inner_r * HALF, HALF * HALF]
    starts, at = [], 0
    for size in sizes:
        starts.append(at)
        at += up(size, 16)
    return sizes, starts, at


def tile_sizes(row_count, col_count):
    sizes = [row_count * col_count] + piece_sizes(row_count, col_count)[0][1:]
    starts, at = [], 0
    for size in sizes:
        starts.append(at)
        at += up(size, 16)
    return sizes, starts, at


def roll_send(row_count, col_count):
    inner_c = col_count - HALF
    _, starts, total = piece_sizes(row_count, col_count)
    base = starts[1]
    table = np.zeros((total - base, row_count * col_count), np.float32)
    for i in range(row_count):
        for j in range(col_count):
            low = i - (row_count - HALF)
            if low >= 0 and j >= HALF:
                target = starts[1] + low * inner_c + (j - HALF)
            elif low >= 0:
                target = starts[3] + low * HALF + j
            elif j < HALF:
                target = starts[2] + i * HALF + j
            else:
                continue
            table[target - base, i * col_count + j] = 1.0
    return table


def roll_gather(row_count, col_count):
    inner_c = col_count - HALF
    _, starts, total = tile_sizes(row_count, col_count)
    table = np.zeros((row_count * col_count, total), np.float32)
    for token, (i, j) in enumerate(window_order(row_count, col_count)):
        if i >= HALF and j < inner_c:
            source = starts[0] + (i - HALF) * col_count + (j + HALF)
        elif j < inner_c:
            source = starts[1] + i * inner_c + j
        elif i >= HALF:
            source = starts[2] + (i - HALF) * HALF + (j - inner_c)
        else:
            source = starts[3] + i * HALF + (j - inner_c)
        table[token, source] = 1.0
    return table


def unroll_scatter(row_count, col_count):
    inner_c = col_count - HALF
    _, starts, total = piece_sizes(row_count, col_count)
    table = np.zeros((total, row_count * col_count), np.float32)
    for token, (i, j) in enumerate(window_order(row_count, col_count)):
        if i >= HALF and j < inner_c:
            target = starts[0] + (i - HALF) * inner_c + j
        elif j < inner_c:
            target = starts[1] + i * inner_c + j
        elif i >= HALF:
            target = starts[2] + (i - HALF) * HALF + (j - inner_c)
        else:
            target = starts[3] + i * HALF + (j - inner_c)
        table[target, token] = 1.0
    return table


def unroll_gather(row_count, col_count):
    inner_r, inner_c = row_count - HALF, col_count - HALF
    _, starts, total = piece_sizes(row_count, col_count)
    table = np.zeros((row_count * col_count, total), np.float32)
    for i in range(row_count):
        for j in range(col_count):
            if i < inner_r and j >= HALF:
                source = starts[0] + i * inner_c + (j - HALF)
            elif j >= HALF:
                source = starts[1] + (i - inner_r) * inner_c + (j - HALF)
            elif i < inner_r:
                source = starts[2] + i * HALF + j
            else:
                source = starts[3] + (i - inner_r) * HALF + j
            table[i * col_count + j, source] = 1.0
    return table


def cell_list():
    cells = []
    for s in bin_scales:
        for a in range(s):
            for b in range(s):
                cells.append((s, a, b))
    return cells


CELLS = cell_list()
NCELL = len(CELLS)
FINE = bin_scales[-1]
NFINE = FINE * FINE
FINE_PAD = up(NFINE, 8)
SENT = [k for k, (s, _, _) in enumerate(CELLS) if s == FINE or (s > 1 and (FINE // s) % 2 == 0)]
NSENT = len(SENT)
CELL_PAD = up(NSENT + 1, 8)


def cell_table(height, breadth, sent):
    chosen = [CELLS[k] for k in SENT] if sent else CELLS
    table = np.zeros((64, 8), np.float32)
    for k, (s, a, b) in enumerate(chosen):
        table[k, :5] = (s / height, s / breadth, s - 1.0, a, b)
    table[len(chosen) :, 3] = -9.0
    return table


def spread_table():
    table = np.zeros((64, CELL_PAD), np.float32)
    for k, (s, a, b) in enumerate(CELLS):
        if k in SENT:
            table[k, SENT.index(k)] = 1.0
            continue
        for m, sent in enumerate(SENT):
            t, aa, bb = CELLS[sent]
            if t == FINE:
                row = np.clip((aa + 0.5) * s / FINE - 0.5, 0.0, s - 1.0)
                col = np.clip((bb + 0.5) * s / FINE - 0.5, 0.0, s - 1.0)
                table[k, m] = max(0.0, 1.0 - abs(row - a)) * max(0.0, 1.0 - abs(col - b))
    return table


def fine_table(height, breadth):
    table = np.zeros((FINE_PAD, 8), np.float32)
    table[:, :4] = -1.0
    for a in range(FINE):
        for b in range(FINE):
            table[a * FINE + b, :4] = (
                a * (height // FINE),
                (a + 1) * (height // FINE),
                b * (breadth // FINE),
                (b + 1) * (breadth // FINE),
            )
    return table


def cell_slots():
    slots, at = [], 0
    for s in bin_scales:
        slots.append((at, up(s * s, 8)))
        at += up(s * s, 8)
    return slots, at


def group_table():
    slots, total = cell_slots()
    table = np.zeros((total, FINE_PAD), np.float32)
    for (first, _), s in zip(slots, bin_scales):
        step = FINE // s
        for a in range(s):
            for b in range(s):
                for aa in range(a * step, (a + 1) * step):
                    for bb in range(b * step, (b + 1) * step):
                        table[first + a * s + b, aa * FINE + bb] = 1.0
    return np.concatenate([table] * 3, 1)


def spread_weights(total, s):
    place = np.clip((np.arange(total) + 0.5) * s / total - 0.5, 0.0, s - 1.0)
    return np.maximum(0.0, 1.0 - np.abs(place[:, None] - np.arange(s)[None, :]))


def gram_tables(height, breadth):
    rows = np.zeros((height, 64))
    cols = np.zeros((breadth, 64))
    for k, (s, a, b) in enumerate(CELLS):
        rows[:, k] = spread_weights(height, s)[:, a]
        cols[:, k] = spread_weights(breadth, s)[:, b]
    gram = (rows.T @ rows) * (cols.T @ cols)
    mass = rows.sum(0) * cols.sum(0)
    gram[NCELL] = mass
    both = np.zeros((up(64 + CELL_PAD, 16), 64))
    both[:64] = gram
    both[64 : 64 + NSENT] = spread_table().T[:NSENT]
    parts = []
    for _ in range(3):
        part = both.astype(jnp.bfloat16).astype(np.float64)
        parts.append(part)
        both = both - part
    table = np.concatenate(parts, 0)
    return np.concatenate([table] * 3, 1).astype(np.float32)


def send_kernel(
    geo, tokens_ref, table_ref, rel_ref, rr_ref, rc_ref, rd_ref, rel_out_ref, tok_ref, tab_ref, sem
):
    sizes, starts, _ = piece_sizes(geo[0], geo[1])
    copies = [
        pltpu.make_async_copy(tokens_ref, tok_ref, sem.at[0]),
        pltpu.make_async_copy(table_ref, tab_ref, sem.at[1]),
        pltpu.make_async_copy(rel_ref, rel_out_ref, sem.at[2]),
    ]
    for copy in copies:
        copy.start()
    for copy in copies:
        copy.wait()
    pieces = contract(tab_ref[...], tok_ref[...], ((1,), (0,))).astype(bf16)
    for ref, start, size in zip((rr_ref, rc_ref, rd_ref), starts[1:], sizes[1:]):
        at = start - starts[1]
        ref[...] = pieces[at : at + size]


def bias_kernel(count, table_ref, *refs):
    sources, out_ref = refs[:count], refs[count]
    targets = refs[count + 1 : 2 * count + 1]
    line_ref, sem = refs[2 * count + 1 :]
    copies = [
        pltpu.make_async_copy(source, target, sem.at[k])
        for k, (source, target) in enumerate(zip(sources, targets))
    ]
    for copy in copies:
        copy.start()
    heads = table_ref.shape[2]
    span = 2 * WIN - 1
    line_ref[...] = jnp.zeros_like(line_ref)
    for a in range(span):
        line_ref[a % 2, :, WIN * a : WIN * a + span] = table_ref[a].T
    wide = [
        [
            jnp.broadcast_to(line_ref[par, :, 128 * t : 128 * t + 128][:, None, :], (heads, 8, 128))
            for t in range(3)
        ]
        for par in range(2)
    ]
    lane = lax.broadcasted_iota(jnp.int32, (8, 128), 1)
    sub = lax.broadcasted_iota(jnp.int32, (8, 128), 0)
    tail = WIN * WIN - 128
    per_slot = 128 // tail
    blocks = WIN * WIN // 8

    def move(k):
        base = WIN * WIN - 8 - 8 * k
        tile, rest = base // 128, base % 128
        last = tile + 3 if rest + 7 + tail > 128 else tile + 2
        return [
            [
                pltpu.roll(wide[par][t], 121 - rest, 2, stride=1, stride_axis=1)
                for t in range(tile, last)
            ]
            for par in range(2)
        ]

    def choose(k, moved):
        near = (lane < 121 - (WIN * WIN - 8 - 8 * k) % 128 + sub)[None]
        u = (8 * k + sub) // WIN
        rows = slice(8 * k, 8 * k + 8)
        odd = ((lane // WIN + u) % 2 == 1)[None]
        main = jnp.where(
            odd, jnp.where(near, *moved[0][:2]), jnp.where(near, *moved[1][:2])
        )
        rest = [m[1] if len(m) == 2 else jnp.where(near, *m[1:]) for m in moved]
        odd = (((128 + lane) // WIN + u) % 2 == 1)[None]
        part = jnp.where((lane < tail)[None], jnp.where(odd, *rest), 0.0)
        for g in range(heads // per_slot):
            slot = g * (per_slot + 1)
            out_ref[slot : slot + per_slot, rows, :] = main[g * per_slot : (g + 1) * per_slot]
        return [
            part[h] if h % per_slot == 0 else pltpu.roll(part[h], tail * (h % per_slot), 1)
            for h in range(heads)
        ]

    def join(k, pieces):
        for g in range(heads // per_slot):
            mine = pieces[g * per_slot : (g + 1) * per_slot]
            while len(mine) > 1:
                mine = [x + y for x, y in zip(mine[::2], mine[1::2])]
            out_ref[g * (per_slot + 1) + per_slot, 8 * k : 8 * k + 8, :] = mine[0]

    moved, pieces = {}, {}
    for k in range(blocks + 2):
        if k < blocks:
            moved[k] = move(k)
        if 0 <= k - 1 < blocks:
            pieces[k - 1] = choose(k - 1, moved.pop(k - 1))
        if 0 <= k - 2:
            join(k - 2, pieces.pop(k - 2))
    for copy in copies:
        copy.wait()


def expanded_bias(rel_table, *brought):
    heads = rel_table.shape[2]
    tokens = WIN * WIN
    vmem = pl.BlockSpec(memory_space=pltpu.VMEM)
    return pl.pallas_call(
        functools.partial(bias_kernel, len(brought)),
        out_shape=[jax.ShapeDtypeStruct((heads // GROUP * (GROUP + 1), tokens, 128), f32)]
        + [jax.ShapeDtypeStruct(x.shape, x.dtype) for x in brought],
        in_specs=[vmem] + [pl.BlockSpec(memory_space=pltpu.HBM)] * len(brought),
        out_specs=[vmem] * (1 + len(brought)),
        scratch_shapes=[
            pltpu.VMEM((2, heads, 384), f32),
            pltpu.SemaphoreType.DMA((len(brought),)),
        ],
        compiler_params=pltpu.CompilerParams(vmem_limit_bytes=16 << 20),
        cost_estimate=pl.CostEstimate(
            flops=4 * heads * tokens * tokens,
            bytes_accessed=4 * heads * tokens * 144,
            transcendentals=0,
        ),
        name="expand_bias",
    )(rel_table, *[pltpu.with_memory_space_constraint(x, pltpu.HBM) for x in brought])


def contract(a, b, dims, **kw):
    return lax.dot_general(a, b, (dims, ((), ())), preferred_element_type=f32, **kw)


def f32_parts(value):
    first = value.astype(bf16).astype(f32)
    rest = value - first
    second = rest.astype(bf16).astype(f32)
    return [first, second, (rest - second).astype(bf16).astype(f32)]


def folded(value):
    count = value.shape[0] // 3
    return value[:count] + (value[count : 2 * count] + value[2 * count :])


def attention_kernel(
    geo,
    own_ref,
    rr_ref,
    rc_ref,
    rd_ref,
    gather_ref,
    far_scatter_ref,
    lng_ref,
    lnb_ref,
    wqkv_ref,
    bqkv_ref,
    bias_ref,
    far_proj_ref,
    bproj_ref,
    far_join_ref,
    small_ref,
    keep_ref,
    send_ref,
    o_own_ref,
    o_row_ref,
    o_col_ref,
    o_diag_ref,
    xs_ref,
    q_ref,
    k_ref,
    vt_ref,
    ct_ref,
    blk_ref,
    pen_ref,
    buf_ref,
    sa_ref,
    sb_ref,
    pa_ref,
    pb_ref,
    wproj_ref,
    wjoin_ref,
    scatter_ref,
    sem,
):
    copies = [
        pltpu.make_async_copy(far_proj_ref, wproj_ref, sem.at[0]),
        pltpu.make_async_copy(far_join_ref, wjoin_ref, sem.at[1]),
        pltpu.make_async_copy(far_scatter_ref, scatter_ref, sem.at[2]),
    ]
    for copy in copies:
        copy.start()
    row_count, col_count, height, breadth = geo
    nwr, nwc = row_count // WIN, col_count // WIN
    tokens, width = row_count * col_count, own_ref.shape[1]
    wt = WIN * WIN
    heads = bias_ref.shape[0] // (GROUP + 1) * GROUP
    hd = width // heads
    per_tile = 128 // hd
    my_row, my_col = lax.axis_index("rows"), lax.axis_index("cols")
    bit = lax.rem(my_col, 2)
    sizes, starts, total = tile_sizes(row_count, col_count)
    xs_ref[starts[1] :, :] = jnp.zeros((total - starts[1], width), bf16)
    for ref, start, size in zip((own_ref, rr_ref, rc_ref, rd_ref), starts, sizes):
        xs_ref[start : start + size, :] = ref[...]
    sizes, starts, total = piece_sizes(row_count, col_count)
    rolled = contract(gather_ref[...], xs_ref[...], ((1,), (0,)))
    center = jnp.mean(rolled, -1, keepdims=True)
    delta = rolled - center
    spread = jnp.mean(delta * delta, -1, keepdims=True)
    normed = (delta * lax.rsqrt(spread + norm_eps) * lng_ref[...][None, :] + lnb_ref[...][None, :]).astype(bf16)
    blk_ref[...] = rolled.astype(bf16)
    for part in range(3):
        cols = slice(part * width, (part + 1) * width)
        mixed = contract(normed, wqkv_ref[:, cols], ((1,), (0,))) + bqkv_ref[cols][None, :]
        if part == 0:
            q_ref[...] = (mixed * hd ** (-0.5)).astype(bf16).reshape(q_ref.shape)
        elif part == 1:
            k_ref[...] = mixed.astype(bf16).reshape(k_ref.shape)
        else:
            for w in range(nwr * nwc):
                vt_ref[w] = mixed[w * wt : (w + 1) * wt].T.astype(bf16)

    sub = lax.broadcasted_iota(jnp.int32, (wt, 128), 0)
    lane = lax.broadcasted_iota(jnp.int32, (wt, 128), 1)
    for kind, query in enumerate((lane, 128 + lane % TAIL)):
        row_diff = (sub < wt // 2) != (query < wt // 2)
        col_diff = (sub % WIN < HALF) != (query % WIN < HALF)
        for wr in range(nwr):
            for wc in range(nwc):
                row_last = my_row * nwr + wr == 0
                col_last = my_col * nwc + wc == breadth // WIN - 1
                bad = (row_diff & row_last) | (col_diff & col_last)
                pen_ref[kind, wr * nwc + wc] = jnp.where(bad, -100.0, 0.0)

    head_lane = lax.broadcasted_iota(jnp.int32, (wt, 128), 1) // hd
    span = GROUP * hd
    joint_shape = (GROUP * TAIL, span)
    joint_own = (
        lax.broadcasted_iota(jnp.int32, joint_shape, 0) // TAIL
        == lax.broadcasted_iota(jnp.int32, joint_shape, 1) // hd
    )
    groups = heads // GROUP
    steps = nwr * nwc * groups

    def make_scores(step, s_ref):
        step = jnp.minimum(step, steps - 1)
        w, g = step // groups, step % groups
        for h in range(GROUP):
            at = pl.multiple_of(g * span + h // per_tile * 128, 128)
            keys = k_ref[w, :, pl.ds(at, 128)]
            keys = jnp.where(head_lane == h % per_tile, keys, jnp.zeros_like(keys))
            s_ref[h] = contract(keys, q_ref[w, :128, pl.ds(at, 128)], ((1,), (1,)))
        at = pl.multiple_of(g * span, span)
        joint = jnp.concatenate([q_ref[w, 128:, pl.ds(at, span)]] * GROUP, 0)
        joint = jnp.where(joint_own, joint, jnp.zeros_like(joint))
        s_ref[GROUP] = contract(k_ref[w, :, pl.ds(at, span)], joint, ((1,), (1,)))

    def make_weights(step, s_ref, p_ref):
        w, g = step // groups, step % groups
        for h in range(GROUP + 1):
            scores = s_ref[h] + bias_ref[g * (GROUP + 1) + h] + pen_ref[h // GROUP, w]
            top = jnp.max(scores, 0, keepdims=True)
            grown = jnp.exp(scores - top)
            scale = 1.0 / jnp.sum(grown, 0, keepdims=True)
            p_ref[h] = (grown * scale).astype(bf16)

    def make_context(step, p_ref):
        step = jnp.maximum(step, 0)
        w, g = step // groups, step % groups
        first = pl.multiple_of(g * span, span)
        joint = contract(vt_ref[w, pl.ds(first, span), :], p_ref[GROUP], ((1,), (0,)))
        for h in range(GROUP):
            place = pl.multiple_of(first + h * hd, hd)
            context = contract(vt_ref[w, pl.ds(place, hd), :], p_ref[h], ((1,), (0,)))
            ct_ref[w, pl.ds(place, hd), :128] = context.astype(bf16)
            rest = joint[h * hd : (h + 1) * hd]
            if h:
                rest = pltpu.roll(rest, 128 - TAIL * h, 1)
            ct_ref[w, pl.ds(place, hd), 128:] = rest[:, :TAIL].astype(bf16)

    def step_pair(pair, carry):
        step = pair * 2
        make_scores(step + 1, sb_ref)
        make_weights(step, sa_ref, pa_ref)
        make_context(step - 1, pb_ref)
        make_scores(step + 2, sa_ref)
        make_weights(step + 1, sb_ref, pb_ref)
        make_context(step, pa_ref)
        return carry

    make_scores(0, sa_ref)
    lax.fori_loop(0, steps // 2, step_pair, 0)
    make_context(steps - 1, pb_ref)

    for copy in copies:
        copy.wait()
    for w in range(nwr * nwc):
        attended = contract(ct_ref[w], wproj_ref[...], ((0,), (0,))) + bproj_ref[...][None, :]
        here = slice(w * wt, (w + 1) * wt)
        blk_ref[here, :] = (blk_ref[here, :].astype(f32) + attended).astype(bf16)

    block = blk_ref[...]
    pieces = contract(scatter_ref[...], block, ((1,), (0,))).astype(bf16)
    for ref, start, size in zip((o_own_ref, o_row_ref, o_col_ref, o_diag_ref), starts, sizes):
        ref[...] = pieces[start : start + size]

    row = small_ref[0:1, :tokens] + (my_row * row_count - HALF).astype(f32)
    col = small_ref[1:2, :tokens] + (my_col * col_count + HALF).astype(f32)
    row = jnp.where(row < 0, row + height, row)
    col = jnp.where(col >= breadth, col - breadth, col)
    fine = small_ref[72 : 72 + FINE_PAD, :8]
    inside = (
        (row >= fine[:, 0:1]) & (row < fine[:, 1:2]) & (col >= fine[:, 2:3]) & (col < fine[:, 3:4])
    )
    cell = small_ref[8 : 8 + CELL_PAD, :8]
    row_at = jnp.clip((row + 0.5) * cell[:, 0:1] - 0.5, 0.0, cell[:, 2:3])
    col_at = jnp.clip((col + 0.5) * cell[:, 1:2] - 0.5, 0.0, cell[:, 2:3])
    share = jnp.maximum(0.0, 1.0 - jnp.abs(row_at - cell[:, 3:4])) * jnp.maximum(
        0.0, 1.0 - jnp.abs(col_at - cell[:, 4:5])
    )
    picks = jnp.concatenate([inside.astype(f32), *f32_parts(share)], 0).astype(bf16)
    picked = contract(picks, block, ((1,), (0,)))
    pooled = picked[:FINE_PAD]
    lifted = folded(picked[FINE_PAD:])
    both = jnp.concatenate([block, jnp.concatenate(f32_parts(lifted), 0).astype(bf16)], 0)
    joined = contract(both, wjoin_ref[...], ((1,), (0,)))
    direct, weighted = joined[:tokens], folded(joined[tokens:])
    squares = jnp.sum(direct * direct, 0, keepdims=True)
    which = lax.broadcasted_iota(jnp.int32, weighted.shape, 0)
    weighted = jnp.where(which == NSENT, squares, weighted)
    half_w, half_c = width // 2, direct.shape[1] // 2
    for b in range(2):
        at = 0
        for t in range(half_w // 128):
            lo = b * half_w + t * 128
            buf_ref[b, at : at + NFINE, :] = pooled[:NFINE, lo : lo + 128]
            at += NFINE
        for t in range(half_c // 128):
            lo = b * half_c + t * 128
            buf_ref[b, at : at + NSENT + 1, :] = weighted[: NSENT + 1, lo : lo + 128]
            at += NSENT + 1
        if at < buf_ref.shape[1]:
            buf_ref[b, at:, :] = jnp.zeros((buf_ref.shape[1] - at, 128), f32)
    keep_ref[...] = buf_ref[bit]
    send_ref[...] = buf_ref[1 - bit]


def half_rows(width, channels):
    return up(NFINE * (width // 256) + (NSENT + 1) * (channels // 256), 8)


def direct_kernel(
    geo, own_ref, rr_ref, rc_ref, rd_ref, gather_ref, wjoin_ref, token_ref, cell_ref,
    out_ref, share_ref, xs_ref
):
    row_count, col_count, _, _ = geo
    sizes, starts, _ = piece_sizes(row_count, col_count)
    my_row, my_col = lax.axis_index("rows"), lax.axis_index("cols")
    xs_ref[...] = jnp.zeros_like(xs_ref)
    for ref, start, size in zip((own_ref, rr_ref, rc_ref, rd_ref), starts, sizes):
        xs_ref[start : start + size, :] = ref[...]
    block = contract(gather_ref[...], xs_ref[...], ((1,), (0,))).astype(bf16)
    out_ref[...] = contract(block, wjoin_ref[...], ((1,), (0,)))
    row = token_ref[:, 0:1] + (my_row * row_count).astype(f32)
    col = token_ref[:, 1:2] + (my_col * col_count).astype(f32)
    row_at = jnp.clip((row + 0.5) * cell_ref[0:1, :] - 0.5, 0.0, cell_ref[2:3, :])
    col_at = jnp.clip((col + 0.5) * cell_ref[1:2, :] - 0.5, 0.0, cell_ref[2:3, :])
    share = jnp.maximum(0.0, 1.0 - jnp.abs(row_at - cell_ref[3:4, :])) * jnp.maximum(
        0.0, 1.0 - jnp.abs(col_at - cell_ref[4:5, :])
    )
    upper = share.astype(bf16)
    lower = (share - upper.astype(f32)).astype(bf16)
    share_ref[:, :128] = upper
    share_ref[:, 128:] = lower


def two_part_dot(value, weight):
    first = value.astype(bf16).astype(f32)
    parts = jnp.concatenate([first, value - first], 0).astype(bf16)
    product = contract(parts, weight, ((1,), (0,)))
    return product[: value.shape[0]] + product[value.shape[0] :]


def final_kernel(
    geo,
    mine_ref,
    other_ref,
    direct_ref,
    share_ref,
    wb_ref,
    bb_ref,
    jb_ref,
    group_ref,
    gram_ref,
    gain_ref,
    bias_ref,
    out_ref,
    buf_ref,
    pool_ref,
    wei_ref,
    proj_ref,
):
    _, _, height, breadth = geo
    bit = lax.rem(lax.axis_index("cols"), 2)
    width, channels = pool_ref.shape[1], wei_ref.shape[1]
    half_w, half_c = width // 2, channels // 2
    buf_ref[bit] = mine_ref[...]
    buf_ref[1 - bit] = other_ref[...]
    pool_ref[NFINE:, :] = jnp.zeros((pool_ref.shape[0] - NFINE, width), f32)
    wei_ref[NSENT + 1 :, :] = jnp.zeros((wei_ref.shape[0] - NSENT - 1, channels), f32)
    for b in range(2):
        at = 0
        for t in range(half_w // 128):
            lo = b * half_w + t * 128
            pool_ref[:NFINE, lo : lo + 128] = buf_ref[b, at : at + NFINE, :]
            at += NFINE
        for t in range(half_c // 128):
            lo = b * half_c + t * 128
            wei_ref[: NSENT + 1, lo : lo + 128] = buf_ref[b, at : at + NSENT + 1, :]
            at += NSENT + 1
    pool = jnp.concatenate(f32_parts(pool_ref[...]), 0).astype(bf16)
    cells = contract(group_ref[...], pool, ((1,), (0,)))
    proj_ref[...] = jnp.zeros_like(proj_ref)
    start = 0
    for k, (s, (first, count)) in enumerate(zip(bin_scales, cell_slots()[0])):
        scale = 1.0 / float((height // s) * (breadth // s))
        hidden = two_part_dot(cells[first : first + count] * scale, wb_ref[k])
        hidden = jnp.maximum(hidden + bb_ref[k : k + 1, :], 0.0)
        lift = two_part_dot(hidden, jb_ref[k])
        proj_ref[start : start + s * s, :] = lift[: s * s]
        start += s * s
    projected = proj_ref[...]
    parts = [part.astype(bf16) for part in f32_parts(projected)]
    everyone = float(height * breadth)
    spun = folded(contract(gram_ref[...], jnp.concatenate(parts, 0), ((1,), (0,))))
    weighted = wei_ref[...]
    which = lax.broadcasted_iota(jnp.int32, weighted.shape, 0)
    finest = jnp.where((which >= NSENT - NFINE) & (which < NSENT), weighted, 0.0)
    mean_val = (jnp.sum(finest, 0, keepdims=True) + spun[NCELL : NCELL + 1]) * (1.0 / everyone)
    cross = jnp.sum(weighted * spun[64 : 64 + CELL_PAD], 0, keepdims=True)
    square = jnp.sum(projected * spun[:64], 0, keepdims=True)
    variance = (weighted[NSENT : NSENT + 1] + 2.0 * cross + square) * (
        1.0 / everyone
    ) - mean_val * mean_val
    scale = lax.rsqrt(variance + norm_eps) * gain_ref[...][None, :]
    stack = jnp.concatenate(parts[:2] * 2, 0)
    lifted = contract(share_ref[...], stack, ((1,), (0,)))
    joined = (direct_ref[...] + lifted - mean_val) * scale + bias_ref[...][None, :]
    out_ref[...] = jnp.maximum(joined, 0.0).astype(bf16)


def shards(
    tokens,
    ln_gain,
    ln_bias,
    qkv_weight,
    qkv_bias,
    rel_table,
    proj_weight,
    proj_bias,
    branch_weight,
    branch_bias,
    join_block,
    join_branch,
    bn_gain,
    bn_bias,
):
    row_count, col_count, width = tokens.shape
    nrow, ncol = lax.axis_size("rows"), lax.axis_size("cols")
    height, breadth = row_count * nrow, col_count * ncol
    geo = (row_count, col_count, height, breadth)
    channels = join_block.shape[1]
    count = row_count * col_count
    nwin = count // (WIN * WIN)
    everyone = nrow * ncol
    sizes, _, total = piece_sizes(row_count, col_count)

    def shifted(value, down, right):
        pairs = []
        for r in range(nrow):
            for c in range(ncol):
                pairs.append(
                    (r * ncol + c, ((r + down) % nrow) * ncol + (c + right) % ncol)
                )
        return lax.ppermute(value, axes, pairs)

    def exchanged(value, masks):
        return lax.ppermute(value, axes, [(i, i ^ masks[i % 2]) for i in range(everyone)])

    vmem = pl.BlockSpec(memory_space=pltpu.VMEM)
    hbm = pl.BlockSpec(memory_space=pltpu.HBM)

    shape = jax.ShapeDtypeStruct
    own = tokens.reshape(count, width)
    send_table = roll_send(row_count, col_count)
    send_rr, send_rc, send_rd, near_rel = pl.pallas_call(
        functools.partial(send_kernel, geo),
        out_shape=[shape((size, width), bf16) for size in sizes[1:]]
        + [shape(rel_table.shape, rel_table.dtype)],
        in_specs=[hbm] * 3,
        out_specs=[vmem] * 4,
        scratch_shapes=[
            pltpu.VMEM((count, width), bf16),
            pltpu.VMEM(send_table.shape, bf16),
            pltpu.SemaphoreType.DMA((3,)),
        ],
        compiler_params=pltpu.CompilerParams(vmem_limit_bytes=8 << 20),
        name="send_pieces",
    )(
        pltpu.with_memory_space_constraint(own, pltpu.HBM),
        pltpu.with_memory_space_constraint(jnp.asarray(send_table, bf16), pltpu.HBM),
        pltpu.with_memory_space_constraint(rel_table, pltpu.HBM),
    )
    rr = shifted(send_rr, 1, 0)
    rd = shifted(send_rd, 1, -1)
    rc = shifted(send_rc, 0, -1)

    order = np.array(window_order(row_count, col_count), np.float32)
    token_lanes = np.zeros((8, count), np.float32)
    token_lanes[:2] = order.T
    grid = np.zeros((count, 8), np.float32)
    grid[:, 0] = np.arange(count) // col_count
    grid[:, 1] = np.arange(count) % col_count
    cells = cell_table(height, breadth, False)
    sent_cells = cell_table(height, breadth, True)
    cell_lanes = np.zeros((8, 128), np.float32)
    cell_lanes[:, :64] = cells.T
    cell_lanes[:, 64:] = cells.T
    rows_half = half_rows(width, channels)

    small = np.zeros((128, 384), np.float32)
    small[:8, :count] = token_lanes
    small[8:72, :8] = sent_cells
    small[72 : 72 + FINE_PAD, :8] = fine_table(height, breadth)
    pair_bias, near_qkv, near_gather, near_small, near_own = expanded_bias(
        near_rel,
        qkv_weight,
        jnp.asarray(roll_gather(row_count, col_count), bf16),
        jnp.asarray(small),
        own,
    )
    scatter = jnp.asarray(unroll_scatter(row_count, col_count), bf16)
    keep, send, own_b, row_b, col_b, diag_b = pl.pallas_call(
        functools.partial(attention_kernel, geo),
        out_shape=[
            shape((rows_half, 128), f32),
            shape((rows_half, 128), f32),
        ]
        + [shape((size, width), bf16) for size in sizes],
        in_specs=[vmem] * 5 + [hbm] + [vmem] * 5 + [hbm, vmem, hbm, vmem],
        out_specs=[vmem] * 6,
        scratch_shapes=[
            pltpu.VMEM((tile_sizes(row_count, col_count)[2], width), bf16),
            pltpu.VMEM((nwin, WIN * WIN, width), bf16),
            pltpu.VMEM((nwin, WIN * WIN, width), bf16),
            pltpu.VMEM((nwin, width, WIN * WIN), bf16),
            pltpu.VMEM((nwin, width, WIN * WIN), bf16),
            pltpu.VMEM((count, width), bf16),
            pltpu.VMEM((2, nwin, WIN * WIN, 128), f32),
            pltpu.VMEM((2, rows_half, 128), f32),
            pltpu.VMEM((GROUP + 1, WIN * WIN, 128), f32),
            pltpu.VMEM((GROUP + 1, WIN * WIN, 128), f32),
            pltpu.VMEM((GROUP + 1, WIN * WIN, 128), bf16),
            pltpu.VMEM((GROUP + 1, WIN * WIN, 128), bf16),
            pltpu.VMEM(proj_weight.shape, bf16),
            pltpu.VMEM(join_block.shape, bf16),
            pltpu.VMEM(scatter.shape, bf16),
            pltpu.SemaphoreType.DMA((3,)),
        ],
        compiler_params=pltpu.CompilerParams(vmem_limit_bytes=24 << 20),
        name="window_attention",
    )(
        near_own,
        rr,
        rc,
        rd,
        near_gather,
        pltpu.with_memory_space_constraint(scatter, pltpu.HBM),
        ln_gain,
        ln_bias,
        near_qkv,
        qkv_bias,
        pair_bias,
        pltpu.with_memory_space_constraint(proj_weight, pltpu.HBM),
        proj_bias,
        pltpu.with_memory_space_constraint(join_block, pltpu.HBM),
        near_small,
    )

    rr_b = shifted(row_b, -1, 0)
    rd_b = shifted(diag_b, -1, 1)
    rc_b = shifted(col_b, 0, 1)
    mine = keep + exchanged(send, (1, 1))
    for masks in round_masks(everyone):
        mine = mine + exchanged(mine, masks)
    other = exchanged(mine, (1, 1))

    direct, share = pl.pallas_call(
        functools.partial(direct_kernel, geo),
        out_shape=[shape((count, channels), f32), shape((count, 256), bf16)],
        in_specs=[vmem] * 8,
        out_specs=[vmem] * 2,
        scratch_shapes=[pltpu.VMEM((total, width), bf16)],
        compiler_params=pltpu.CompilerParams(vmem_limit_bytes=16 << 20),
        cost_estimate=pl.CostEstimate(
            flops=2 * count * width * channels, bytes_accessed=4 << 20, transcendentals=0
        ),
        name="direct_join",
    )(
        own_b,
        rr_b,
        rc_b,
        rd_b,
        jnp.asarray(unroll_gather(row_count, col_count), bf16),
        join_block,
        jnp.asarray(grid),
        jnp.asarray(cell_lanes),
    )

    joined = pl.pallas_call(
        functools.partial(final_kernel, geo),
        out_shape=shape((count, channels), bf16),
        in_specs=[vmem] * 11,
        out_specs=vmem,
        scratch_shapes=[
            pltpu.VMEM((2, rows_half, 128), f32),
            pltpu.VMEM((FINE_PAD, width), f32),
            pltpu.VMEM((CELL_PAD, channels), f32),
            pltpu.VMEM((64, channels), f32),
        ],
        compiler_params=pltpu.CompilerParams(vmem_limit_bytes=24 << 20),
        name="final_join",
    )(
        mine,
        other,
        direct,
        share,
        branch_weight,
        branch_bias,
        join_branch,
        jnp.asarray(group_table(), bf16),
        jnp.asarray(gram_tables(height, breadth), bf16),
        bn_gain,
        bn_bias,
    )
    return joined.reshape(row_count, col_count, channels)


def round_masks(count):
    masks = [1 << k for k in range(1, count.bit_length() - 1)]
    half = len(masks) // 2
    rounds = []
    for first, second in zip(masks[:half], masks[half : 2 * half]):
        rounds += [(first, second), (second, first)]
    return rounds + [(mask, mask) for mask in masks[2 * half :]]


def solution(mesh):
    in_specs = (P("rows", "cols", None),) + (P(),) * 13
    return jax.shard_map(
        shards, mesh=mesh, in_specs=in_specs, out_specs=P("rows", "cols", None), check_vma=False
    )
```

```python
import functools

import jax
import jax.numpy as jnp
import numpy as np
from jax import lax
from jax.experimental import pallas as pl
from jax.experimental.pallas import tpu as pltpu
from jax.sharding import PartitionSpec as P


WIN = 12
HALF = WIN // 2
bin_scales = (1, 2, 3, 6)
norm_eps = 1e-05
f32 = jnp.float32
bf16 = jnp.bfloat16
axes = ("rows", "cols")
TAIL = WIN * WIN - 128
GROUP = 128 // TAIL


def up(count, step):
    return -(-count // step) * step


def window_order(row_count, col_count):
    order = []
    for wr in range(row_count // WIN):
        for wc in range(col_count // WIN):
            for p in range(WIN):
                for q in range(WIN):
                    order.append((wr * WIN + p, wc * WIN + q))
    return order


def piece_sizes(row_count, col_count):
    inner_r, inner_c = row_count - HALF, col_count - HALF
    sizes = [inner_r * inner_c, HALF * inner_c, inner_r * HALF, HALF * HALF]
    starts, at = [], 0
    for size in sizes:
        starts.append(at)
        at += up(size, 16)
    return sizes, starts, at


def tile_sizes(row_count, col_count):
    sizes = [row_count * col_count] + piece_sizes(row_count, col_count)[0][1:]
    starts, at = [], 0
    for size in sizes:
        starts.append(at)
        at += up(size, 16)
    return sizes, starts, at


def roll_send(row_count, col_count):
    inner_c = col_count - HALF
    _, starts, total = piece_sizes(row_count, col_count)
    base = starts[1]
    table = np.zeros((total - base, row_count * col_count), np.float32)
    for i in range(row_count):
        for j in range(col_count):
            low = i - (row_count - HALF)
            if low >= 0 and j >= HALF:
                target = starts[1] + low * inner_c + (j - HALF)
            elif low >= 0:
                target = starts[3] + low * HALF + j
            elif j < HALF:
                target = starts[2] + i * HALF + j
            else:
                continue
            table[target - base, i * col_count + j] = 1.0
    return table


def roll_gather(row_count, col_count):
    inner_c = col_count - HALF
    _, starts, total = tile_sizes(row_count, col_count)
    table = np.zeros((row_count * col_count, total), np.float32)
    for token, (i, j) in enumerate(window_order(row_count, col_count)):
        if i >= HALF and j < inner_c:
            source = starts[0] + (i - HALF) * col_count + (j + HALF)
        elif j < inner_c:
            source = starts[1] + i * inner_c + j
        elif i >= HALF:
            source = starts[2] + (i - HALF) * HALF + (j - inner_c)
        else:
            source = starts[3] + i * HALF + (j - inner_c)
        table[token, source] = 1.0
    return table


def unroll_scatter(row_count, col_count):
    inner_c = col_count - HALF
    _, starts, total = piece_sizes(row_count, col_count)
    table = np.zeros((total, row_count * col_count), np.float32)
    for token, (i, j) in enumerate(window_order(row_count, col_count)):
        if i >= HALF and j < inner_c:
            target = starts[0] + (i - HALF) * inner_c + j
        elif j < inner_c:
            target = starts[1] + i * inner_c + j
        elif i >= HALF:
            target = starts[2] + (i - HALF) * HALF + (j - inner_c)
        else:
            target = starts[3] + i * HALF + (j - inner_c)
        table[target, token] = 1.0
    return table


def unroll_gather(row_count, col_count):
    inner_r, inner_c = row_count - HALF, col_count - HALF
    _, starts, total = piece_sizes(row_count, col_count)
    table = np.zeros((row_count * col_count, total), np.float32)
    for i in range(row_count):
        for j in range(col_count):
            if i < inner_r and j >= HALF:
                source = starts[0] + i * inner_c + (j - HALF)
            elif j >= HALF:
                source = starts[1] + (i - inner_r) * inner_c + (j - HALF)
            elif i < inner_r:
                source = starts[2] + i * HALF + j
            else:
                source = starts[3] + (i - inner_r) * HALF + j
            table[i * col_count + j, source] = 1.0
    return table


def differ_tables():
    keys = np.arange(WIN * WIN)[:, None]
    table = np.zeros((2, 2, WIN * WIN, 128), np.float32)
    lanes = np.arange(128)[None, :]
    for kind, query in enumerate((lanes, 128 + lanes % TAIL)):
        table[kind, 0] = (keys // WIN < HALF) != (query // WIN < HALF)
        table[kind, 1] = (keys % WIN < HALF) != (query % WIN < HALF)
    return table


def cell_list():
    cells = []
    for s in bin_scales:
        for a in range(s):
            for b in range(s):
                cells.append((s, a, b))
    return cells


CELLS = cell_list()
NCELL = len(CELLS)
FINE = bin_scales[-1]
NFINE = FINE * FINE
FINE_PAD = up(NFINE, 8)
SENT = [k for k, (s, _, _) in enumerate(CELLS) if s == FINE or (s > 1 and (FINE // s) % 2 == 0)]
NSENT = len(SENT)
CELL_PAD = up(NSENT + 1, 8)


def cell_table(height, breadth, sent):
    chosen = [CELLS[k] for k in SENT] if sent else CELLS
    table = np.zeros((64, 8), np.float32)
    for k, (s, a, b) in enumerate(chosen):
        table[k, :5] = (s / height, s / breadth, s - 1.0, a, b)
    table[len(chosen) :, 3] = -9.0
    return table


def spread_table():
    table = np.zeros((64, CELL_PAD), np.float32)
    for k, (s, a, b) in enumerate(CELLS):
        if k in SENT:
            table[k, SENT.index(k)] = 1.0
            continue
        for m, sent in enumerate(SENT):
            t, aa, bb = CELLS[sent]
            if t == FINE:
                row = np.clip((aa + 0.5) * s / FINE - 0.5, 0.0, s - 1.0)
                col = np.clip((bb + 0.5) * s / FINE - 0.5, 0.0, s - 1.0)
                table[k, m] = max(0.0, 1.0 - abs(row - a)) * max(0.0, 1.0 - abs(col - b))
    return table


def fine_table(height, breadth):
    table = np.zeros((FINE_PAD, 8), np.float32)
    table[:, :4] = -1.0
    for a in range(FINE):
        for b in range(FINE):
            table[a * FINE + b, :4] = (
                a * (height // FINE),
                (a + 1) * (height // FINE),
                b * (breadth // FINE),
                (b + 1) * (breadth // FINE),
            )
    return table


def cell_slots():
    slots, at = [], 0
    for s in bin_scales:
        slots.append((at, up(s * s, 8)))
        at += up(s * s, 8)
    return slots, at


def group_table():
    slots, total = cell_slots()
    table = np.zeros((total, FINE_PAD), np.float32)
    for (first, _), s in zip(slots, bin_scales):
        step = FINE // s
        for a in range(s):
            for b in range(s):
                for aa in range(a * step, (a + 1) * step):
                    for bb in range(b * step, (b + 1) * step):
                        table[first + a * s + b, aa * FINE + bb] = 1.0
    return np.concatenate([table] * 3, 1)


def spread_weights(total, s):
    place = np.clip((np.arange(total) + 0.5) * s / total - 0.5, 0.0, s - 1.0)
    return np.maximum(0.0, 1.0 - np.abs(place[:, None] - np.arange(s)[None, :]))


def gram_tables(height, breadth):
    rows = np.zeros((height, 64))
    cols = np.zeros((breadth, 64))
    for k, (s, a, b) in enumerate(CELLS):
        rows[:, k] = spread_weights(height, s)[:, a]
        cols[:, k] = spread_weights(breadth, s)[:, b]
    gram = (rows.T @ rows) * (cols.T @ cols)
    mass = rows.sum(0) * cols.sum(0)
    gram[NCELL] = mass
    both = np.zeros((up(64 + CELL_PAD, 16), 64))
    both[:64] = gram
    both[64 : 64 + NSENT] = spread_table().T[:NSENT]
    parts = []
    for _ in range(3):
        part = both.astype(jnp.bfloat16).astype(np.float64)
        parts.append(part)
        both = both - part
    table = np.concatenate(parts, 0)
    return np.concatenate([table] * 3, 1).astype(np.float32)


def send_kernel(
    geo, tokens_ref, table_ref, rel_ref, rr_ref, rc_ref, rd_ref, rel_out_ref, tok_ref, tab_ref, sem
):
    sizes, starts, _ = piece_sizes(geo[0], geo[1])
    copies = [
        pltpu.make_async_copy(tokens_ref, tok_ref, sem.at[0]),
        pltpu.make_async_copy(table_ref, tab_ref, sem.at[1]),
        pltpu.make_async_copy(rel_ref, rel_out_ref, sem.at[2]),
    ]
    for copy in copies:
        copy.start()
    for copy in copies:
        copy.wait()
    pieces = contract(tab_ref[...], tok_ref[...], ((1,), (0,))).astype(bf16)
    for ref, start, size in zip((rr_ref, rc_ref, rd_ref), starts[1:], sizes[1:]):
        at = start - starts[1]
        ref[...] = pieces[at : at + size]


def bias_kernel(count, table_ref, *refs):
    sources, out_ref = refs[:count], refs[count]
    targets = refs[count + 1 : 2 * count + 1]
    line_ref, sem = refs[2 * count + 1 :]
    copies = [
        pltpu.make_async_copy(source, target, sem.at[k])
        for k, (source, target) in enumerate(zip(sources, targets))
    ]
    for copy in copies:
        copy.start()
    heads = table_ref.shape[2]
    span = 2 * WIN - 1
    line_ref[...] = jnp.zeros_like(line_ref)
    for a in range(span):
        line_ref[a % 2, :, WIN * a : WIN * a + span] = table_ref[a].T
    wide = [
        [
            jnp.broadcast_to(line_ref[par, :, 128 * t : 128 * t + 128][:, None, :], (heads, 8, 128))
            for t in range(3)
        ]
        for par in range(2)
    ]
    lane = lax.broadcasted_iota(jnp.int32, (8, 128), 1)
    sub = lax.broadcasted_iota(jnp.int32, (8, 128), 0)
    tail = WIN * WIN - 128
    per_slot = 128 // tail
    blocks = WIN * WIN // 8

    def move(k):
        base = WIN * WIN - 8 - 8 * k
        tile, rest = base // 128, base % 128
        last = tile + 3 if rest + 7 + tail > 128 else tile + 2
        return [
            [
                pltpu.roll(wide[par][t], 121 - rest, 2, stride=1, stride_axis=1)
                for t in range(tile, last)
            ]
            for par in range(2)
        ]

    def choose(k, moved):
        near = (lane < 121 - (WIN * WIN - 8 - 8 * k) % 128 + sub)[None]
        u = (8 * k + sub) // WIN
        rows = slice(8 * k, 8 * k + 8)
        odd = ((lane // WIN + u) % 2 == 1)[None]
        main = jnp.where(
            odd, jnp.where(near, *moved[0][:2]), jnp.where(near, *moved[1][:2])
        )
        rest = [m[1] if len(m) == 2 else jnp.where(near, *m[1:]) for m in moved]
        odd = (((128 + lane) // WIN + u) % 2 == 1)[None]
        part = jnp.where((lane < tail)[None], jnp.where(odd, *rest), 0.0)
        for g in range(heads // per_slot):
            slot = g * (per_slot + 1)
            out_ref[slot : slot + per_slot, rows, :] = main[g * per_slot : (g + 1) * per_slot]
        return [
            part[h] if h % per_slot == 0 else pltpu.roll(part[h], tail * (h % per_slot), 1)
            for h in range(heads)
        ]

    def join(k, pieces):
        for g in range(heads // per_slot):
            mine = pieces[g * per_slot : (g + 1) * per_slot]
            while len(mine) > 1:
                mine = [x + y for x, y in zip(mine[::2], mine[1::2])]
            out_ref[g * (per_slot + 1) + per_slot, 8 * k : 8 * k + 8, :] = mine[0]

    moved, pieces = {}, {}
    for k in range(blocks + 2):
        if k < blocks:
            moved[k] = move(k)
        if 0 <= k - 1 < blocks:
            pieces[k - 1] = choose(k - 1, moved.pop(k - 1))
        if 0 <= k - 2:
            join(k - 2, pieces.pop(k - 2))
    for copy in copies:
        copy.wait()


def expanded_bias(rel_table, *brought):
    heads = rel_table.shape[2]
    tokens = WIN * WIN
    vmem = pl.BlockSpec(memory_space=pltpu.VMEM)
    return pl.pallas_call(
        functools.partial(bias_kernel, len(brought)),
        out_shape=[jax.ShapeDtypeStruct((heads // GROUP * (GROUP + 1), tokens, 128), f32)]
        + [jax.ShapeDtypeStruct(x.shape, x.dtype) for x in brought],
        in_specs=[vmem] + [pl.BlockSpec(memory_space=pltpu.HBM)] * len(brought),
        out_specs=[vmem] * (1 + len(brought)),
        scratch_shapes=[
            pltpu.VMEM((2, heads, 384), f32),
            pltpu.SemaphoreType.DMA((len(brought),)),
        ],
        compiler_params=pltpu.CompilerParams(vmem_limit_bytes=16 << 20),
        cost_estimate=pl.CostEstimate(
            flops=4 * heads * tokens * tokens,
            bytes_accessed=4 * heads * tokens * 144,
            transcendentals=0,
        ),
        name="expand_bias",
    )(rel_table, *[pltpu.with_memory_space_constraint(x, pltpu.HBM) for x in brought])


def contract(a, b, dims, **kw):
    return lax.dot_general(a, b, (dims, ((), ())), preferred_element_type=f32, **kw)


def f32_parts(value):
    first = value.astype(bf16).astype(f32)
    rest = value - first
    second = rest.astype(bf16).astype(f32)
    return [first, second, (rest - second).astype(bf16).astype(f32)]


def folded(value):
    count = value.shape[0] // 3
    return value[:count] + (value[count : 2 * count] + value[2 * count :])


def attention_kernel(
    geo,
    own_ref,
    rr_ref,
    rc_ref,
    rd_ref,
    gather_ref,
    lng_ref,
    lnb_ref,
    wqkv_ref,
    bqkv_ref,
    bias_ref,
    far_proj_ref,
    bproj_ref,
    far_join_ref,
    small_ref,
    keep_ref,
    send_ref,
    o_block_ref,
    xs_ref,
    q_ref,
    k_ref,
    vt_ref,
    ct_ref,
    blk_ref,
    pen_ref,
    buf_ref,
    sa_ref,
    sb_ref,
    pa_ref,
    pb_ref,
    wproj_ref,
    wjoin_ref,
    sem,
):
    copies = [
        pltpu.make_async_copy(far_proj_ref, wproj_ref, sem.at[0]),
        pltpu.make_async_copy(far_join_ref, wjoin_ref, sem.at[1]),
    ]
    for copy in copies:
        copy.start()
    row_count, col_count, height, breadth = geo
    nwr, nwc = row_count // WIN, col_count // WIN
    tokens, width = row_count * col_count, own_ref.shape[1]
    wt = WIN * WIN
    heads = bias_ref.shape[0] // (GROUP + 1) * GROUP
    hd = width // heads
    per_tile = 128 // hd
    my_row, my_col = lax.axis_index("rows"), lax.axis_index("cols")
    bit = lax.rem(my_col, 2)
    sizes, starts, total = tile_sizes(row_count, col_count)
    xs_ref[starts[1] :, :] = jnp.zeros((total - starts[1], width), bf16)
    for ref, start, size in zip((own_ref, rr_ref, rc_ref, rd_ref), starts, sizes):
        xs_ref[start : start + size, :] = ref[...]
    sizes, starts, total = piece_sizes(row_count, col_count)
    rolled = contract(gather_ref[...], xs_ref[...], ((1,), (0,)))
    center = jnp.mean(rolled, -1, keepdims=True)
    delta = rolled - center
    spread = jnp.mean(delta * delta, -1, keepdims=True)
    normed = (delta * lax.rsqrt(spread + norm_eps) * lng_ref[...][None, :] + lnb_ref[...][None, :]).astype(bf16)
    blk_ref[...] = rolled.astype(bf16)
    for part in (2, 0, 1):
        cols = slice(part * width, (part + 1) * width)
        mixed = contract(normed, wqkv_ref[:, cols], ((1,), (0,))) + bqkv_ref[cols][None, :]
        if part == 0:
            q_ref[...] = (mixed * hd ** (-0.5)).astype(bf16).reshape(q_ref.shape)
        elif part == 1:
            k_ref[...] = mixed.astype(bf16).reshape(k_ref.shape)
        else:
            for w in range(nwr * nwc):
                vt_ref[w] = mixed[w * wt : (w + 1) * wt].T.astype(bf16)

    for wr in range(nwr):
        row_last = jnp.where(my_row * nwr + wr == 0, -100.0, 0.0)
        for wc in range(nwc):
            col_last = jnp.where(my_col * nwc + wc == breadth // WIN - 1, -100.0, 0.0)
            for kind in range(2):
                at = 2 * kind * wt
                pen_ref[kind, wr * nwc + wc] = jnp.minimum(
                    small_ref[at : at + wt] * row_last, small_ref[at + wt : at + 2 * wt] * col_last
                )

    head_lane = lax.broadcasted_iota(jnp.int32, (wt, 128), 1) // hd
    span = GROUP * hd
    joint_shape = (GROUP * TAIL, span)
    joint_own = (
        lax.broadcasted_iota(jnp.int32, joint_shape, 0) // TAIL
        == lax.broadcasted_iota(jnp.int32, joint_shape, 1) // hd
    )
    groups = heads // GROUP
    steps = nwr * nwc * groups

    def make_scores(step, s_ref):
        step = jnp.minimum(step, steps - 1)
        w, g = step // groups, step % groups
        for h in range(GROUP):
            at = pl.multiple_of(g * span + h // per_tile * 128, 128)
            keys = k_ref[w, :, pl.ds(at, 128)]
            keys = jnp.where(head_lane == h % per_tile, keys, jnp.zeros_like(keys))
            s_ref[h] = contract(keys, q_ref[w, :128, pl.ds(at, 128)], ((1,), (1,)))
        at = pl.multiple_of(g * span, span)
        joint = jnp.concatenate([q_ref[w, 128:, pl.ds(at, span)]] * GROUP, 0)
        joint = jnp.where(joint_own, joint, jnp.zeros_like(joint))
        s_ref[GROUP] = contract(k_ref[w, :, pl.ds(at, span)], joint, ((1,), (1,)))

    def make_weights(step, s_ref, p_ref):
        w, g = step // groups, step % groups
        for h in range(GROUP + 1):
            scores = s_ref[h] + bias_ref[g * (GROUP + 1) + h] + pen_ref[h // GROUP, w]
            top = jnp.max(scores, 0, keepdims=True)
            grown = jnp.exp(scores - top)
            scale = 1.0 / jnp.sum(grown, 0, keepdims=True)
            p_ref[h] = (grown * scale).astype(bf16)

    def make_context(step, p_ref):
        step = jnp.maximum(step, 0)
        w, g = step // groups, step % groups
        first = pl.multiple_of(g * span, span)
        joint = contract(vt_ref[w, pl.ds(first, span), :], p_ref[GROUP], ((1,), (0,)))
        for h in range(GROUP):
            place = pl.multiple_of(first + h * hd, hd)
            context = contract(vt_ref[w, pl.ds(place, hd), :], p_ref[h], ((1,), (0,)))
            ct_ref[w, pl.ds(place, hd), :128] = context.astype(bf16)
            rest = joint[h * hd : (h + 1) * hd]
            if h:
                rest = pltpu.roll(rest, 128 - TAIL * h, 1)
            ct_ref[w, pl.ds(place, hd), 128:] = rest[:, :TAIL].astype(bf16)

    def step_pair(pair, carry):
        step = pair * 2
        make_scores(step + 1, sb_ref)
        make_weights(step, sa_ref, pa_ref)
        make_context(step - 1, pb_ref)
        make_scores(step + 2, sa_ref)
        make_weights(step + 1, sb_ref, pb_ref)
        make_context(step, pa_ref)
        return carry

    make_scores(0, sa_ref)
    lax.fori_loop(0, steps // 2, step_pair, 0)
    make_context(steps - 1, pb_ref)

    for copy in copies:
        copy.wait()
    for w in range(nwr * nwc):
        attended = contract(ct_ref[w], wproj_ref[...], ((0,), (0,))) + bproj_ref[...][None, :]
        here = slice(w * wt, (w + 1) * wt)
        blk_ref[here, :] = (blk_ref[here, :].astype(f32) + attended).astype(bf16)

    block = blk_ref[...]
    o_block_ref[...] = block

    cells_at = 4 * wt
    fine_at = cells_at + 64
    place_at = fine_at + FINE_PAD
    lanes = [
        jnp.concatenate(
            [small_ref[at + k : at + k + 1] for at in range(place_at, small_ref.shape[0], 8)], 1
        )[:, :tokens]
        for k in range(2)
    ]
    row = lanes[0] + (my_row * row_count - HALF).astype(f32)
    col = lanes[1] + (my_col * col_count + HALF).astype(f32)
    row = jnp.where(row < 0, row + height, row)
    col = jnp.where(col >= breadth, col - breadth, col)
    fine = small_ref[fine_at : fine_at + FINE_PAD, :8]
    inside = (
        (row >= fine[:, 0:1]) & (row < fine[:, 1:2]) & (col >= fine[:, 2:3]) & (col < fine[:, 3:4])
    )
    cell = small_ref[cells_at : cells_at + CELL_PAD, :8]
    row_at = jnp.clip((row + 0.5) * cell[:, 0:1] - 0.5, 0.0, cell[:, 2:3])
    col_at = jnp.clip((col + 0.5) * cell[:, 1:2] - 0.5, 0.0, cell[:, 2:3])
    share = jnp.maximum(0.0, 1.0 - jnp.abs(row_at - cell[:, 3:4])) * jnp.maximum(
        0.0, 1.0 - jnp.abs(col_at - cell[:, 4:5])
    )
    picks = jnp.concatenate([inside.astype(f32), *f32_parts(share)], 0).astype(bf16)
    picked = contract(picks, block, ((1,), (0,)))
    pooled = picked[:FINE_PAD]
    lifted = folded(picked[FINE_PAD:])
    both = jnp.concatenate([block, jnp.concatenate(f32_parts(lifted), 0).astype(bf16)], 0)
    joined = contract(both, wjoin_ref[...], ((1,), (0,)))
    direct, weighted = joined[:tokens], folded(joined[tokens:])
    squares = jnp.sum(direct * direct, 0, keepdims=True)
    which = lax.broadcasted_iota(jnp.int32, weighted.shape, 0)
    weighted = jnp.where(which == NSENT, squares, weighted)
    half_w, half_c = width // 2, direct.shape[1] // 2
    for b in range(2):
        at = 0
        for t in range(half_w // 128):
            lo = b * half_w + t * 128
            buf_ref[b, at : at + NFINE, :] = pooled[:NFINE, lo : lo + 128]
            at += NFINE
        for t in range(half_c // 128):
            lo = b * half_c + t * 128
            buf_ref[b, at : at + NSENT + 1, :] = weighted[: NSENT + 1, lo : lo + 128]
            at += NSENT + 1
        if at < buf_ref.shape[1]:
            buf_ref[b, at:, :] = jnp.zeros((buf_ref.shape[1] - at, 128), f32)
    keep_ref[...] = buf_ref[bit]
    send_ref[...] = buf_ref[1 - bit]


def half_rows(width, channels):
    return up(NFINE * (width // 256) + (NSENT + 1) * (channels // 256), 8)


def back_kernel(geo, block_ref, table_ref, *out_refs):
    sizes, starts, _ = piece_sizes(geo[0], geo[1])
    pieces = contract(table_ref[...], block_ref[...], ((1,), (0,))).astype(bf16)
    for ref, start, size in zip(out_refs, starts, sizes):
        ref[...] = pieces[start : start + size]


def direct_kernel(
    geo, own_ref, rr_ref, rc_ref, rd_ref, gather_ref, wjoin_ref, token_ref, cell_ref,
    out_ref, share_ref, xs_ref
):
    row_count, col_count, _, _ = geo
    sizes, starts, _ = piece_sizes(row_count, col_count)
    my_row, my_col = lax.axis_index("rows"), lax.axis_index("cols")
    xs_ref[...] = jnp.zeros_like(xs_ref)
    for ref, start, size in zip((own_ref, rr_ref, rc_ref, rd_ref), starts, sizes):
        xs_ref[start : start + size, :] = ref[...]
    block = contract(gather_ref[...], xs_ref[...], ((1,), (0,))).astype(bf16)
    out_ref[...] = contract(block, wjoin_ref[...], ((1,), (0,)))
    row = token_ref[:, 0:1] + (my_row * row_count).astype(f32)
    col = token_ref[:, 1:2] + (my_col * col_count).astype(f32)
    row_at = jnp.clip((row + 0.5) * cell_ref[0:1, :] - 0.5, 0.0, cell_ref[2:3, :])
    col_at = jnp.clip((col + 0.5) * cell_ref[1:2, :] - 0.5, 0.0, cell_ref[2:3, :])
    share = jnp.maximum(0.0, 1.0 - jnp.abs(row_at - cell_ref[3:4, :])) * jnp.maximum(
        0.0, 1.0 - jnp.abs(col_at - cell_ref[4:5, :])
    )
    upper = share.astype(bf16)
    lower = (share - upper.astype(f32)).astype(bf16)
    share_ref[:, :128] = upper
    share_ref[:, 128:] = lower


def two_part_dot(value, weight):
    first = value.astype(bf16).astype(f32)
    parts = jnp.concatenate([first, value - first], 0).astype(bf16)
    product = contract(parts, weight, ((1,), (0,)))
    return product[: value.shape[0]] + product[value.shape[0] :]


def half_hidden(geo, sums_ref, pool_ref, group_ref, wb_ref, half):
    height, breadth = geo[2:]
    wide = pool_ref.shape[1]
    pool_ref[NFINE:, :] = jnp.zeros((pool_ref.shape[0] - NFINE, wide), f32)
    for t in range(wide // 128):
        pool_ref[:NFINE, 128 * t : 128 * t + 128] = sums_ref[NFINE * t : NFINE * t + NFINE, :]
    pool = jnp.concatenate(f32_parts(pool_ref[...]), 0).astype(bf16)
    cells = contract(group_ref[...], pool, ((1,), (0,)))
    rows = pl.ds(pl.multiple_of(half * wide, wide), wide)
    hidden = []
    for k, (s, (first, count)) in enumerate(zip(bin_scales, cell_slots()[0])):
        scale = 1.0 / float((height // s) * (breadth // s))
        hidden.append(two_part_dot(cells[first : first + count] * scale, wb_ref[k, rows, :]))
    return hidden


def half_kernel(geo, mine_ref, wb_ref, group_ref, out_ref, pool_ref):
    half = lax.rem(lax.axis_index("cols"), 2)
    hidden = half_hidden(geo, mine_ref, pool_ref, group_ref, wb_ref, half)
    for part, (first, count) in zip(hidden, cell_slots()[0]):
        out_ref[first : first + count, :] = part


def final_kernel(
    geo,
    half_ref,
    mine_ref,
    other_ref,
    direct_ref,
    share_ref,
    wb_ref,
    bb_ref,
    jb_ref,
    group_ref,
    gram_ref,
    gain_ref,
    bias_ref,
    out_ref,
    buf_ref,
    pool_ref,
    wei_ref,
    proj_ref,
):
    _, _, height, breadth = geo
    bit = lax.rem(lax.axis_index("cols"), 2)
    channels = wei_ref.shape[1]
    half_c = channels // 2
    base = NFINE * (pool_ref.shape[1] // 128)
    buf_ref[bit] = mine_ref[base:, :]
    buf_ref[1 - bit] = other_ref[base:, :]
    wei_ref[NSENT + 1 :, :] = jnp.zeros((wei_ref.shape[0] - NSENT - 1, channels), f32)
    for b in range(2):
        at = 0
        for t in range(half_c // 128):
            lo = b * half_c + t * 128
            wei_ref[: NSENT + 1, lo : lo + 128] = buf_ref[b, at : at + NSENT + 1, :]
            at += NSENT + 1
    second = half_hidden(geo, other_ref, pool_ref, group_ref, wb_ref, 1 - bit)
    proj_ref[...] = jnp.zeros_like(proj_ref)
    start = 0
    for k, (s, (first, count)) in enumerate(zip(bin_scales, cell_slots()[0])):
        hidden = half_ref[first : first + count, :] + second[k]
        hidden = jnp.maximum(hidden + bb_ref[k : k + 1, :], 0.0)
        lift = two_part_dot(hidden, jb_ref[k])
        proj_ref[start : start + s * s, :] = lift[: s * s]
        start += s * s
    projected = proj_ref[...]
    parts = [part.astype(bf16) for part in f32_parts(projected)]
    everyone = float(height * breadth)
    spun = folded(contract(gram_ref[...], jnp.concatenate(parts, 0), ((1,), (0,))))
    weighted = wei_ref[...]
    which = lax.broadcasted_iota(jnp.int32, weighted.shape, 0)
    finest = jnp.where((which >= NSENT - NFINE) & (which < NSENT), weighted, 0.0)
    mean_val = (jnp.sum(finest, 0, keepdims=True) + spun[NCELL : NCELL + 1]) * (1.0 / everyone)
    cross = jnp.sum(weighted * spun[64 : 64 + CELL_PAD], 0, keepdims=True)
    square = jnp.sum(projected * spun[:64], 0, keepdims=True)
    variance = (weighted[NSENT : NSENT + 1] + 2.0 * cross + square) * (
        1.0 / everyone
    ) - mean_val * mean_val
    scale = lax.rsqrt(variance + norm_eps) * gain_ref[...][None, :]
    stack = jnp.concatenate(parts[:2] * 2, 0)
    lifted = contract(share_ref[...], stack, ((1,), (0,)))
    joined = (direct_ref[...] + lifted - mean_val) * scale + bias_ref[...][None, :]
    out_ref[...] = jnp.maximum(joined, 0.0).astype(bf16)


def shards(
    tokens,
    ln_gain,
    ln_bias,
    qkv_weight,
    qkv_bias,
    rel_table,
    proj_weight,
    proj_bias,
    branch_weight,
    branch_bias,
    join_block,
    join_branch,
    bn_gain,
    bn_bias,
):
    row_count, col_count, width = tokens.shape
    nrow, ncol = lax.axis_size("rows"), lax.axis_size("cols")
    height, breadth = row_count * nrow, col_count * ncol
    geo = (row_count, col_count, height, breadth)
    channels = join_block.shape[1]
    count = row_count * col_count
    nwin = count // (WIN * WIN)
    everyone = nrow * ncol
    sizes, _, total = piece_sizes(row_count, col_count)

    def shifted(value, down, right):
        pairs = []
        for r in range(nrow):
            for c in range(ncol):
                pairs.append(
                    (r * ncol + c, ((r + down) % nrow) * ncol + (c + right) % ncol)
                )
        return lax.ppermute(value, axes, pairs)

    def exchanged(value, masks):
        return lax.ppermute(value, axes, [(i, i ^ masks[i % 2]) for i in range(everyone)])

    vmem = pl.BlockSpec(memory_space=pltpu.VMEM)
    hbm = pl.BlockSpec(memory_space=pltpu.HBM)

    shape = jax.ShapeDtypeStruct
    own = tokens.reshape(count, width)
    send_table = roll_send(row_count, col_count)
    send_rr, send_rc, send_rd, near_rel = pl.pallas_call(
        functools.partial(send_kernel, geo),
        out_shape=[shape((size, width), bf16) for size in sizes[1:]]
        + [shape(rel_table.shape, rel_table.dtype)],
        in_specs=[hbm] * 3,
        out_specs=[vmem] * 4,
        scratch_shapes=[
            pltpu.VMEM((count, width), bf16),
            pltpu.VMEM(send_table.shape, bf16),
            pltpu.SemaphoreType.DMA((3,)),
        ],
        compiler_params=pltpu.CompilerParams(vmem_limit_bytes=8 << 20),
        name="send_pieces",
    )(
        pltpu.with_memory_space_constraint(own, pltpu.HBM),
        pltpu.with_memory_space_constraint(jnp.asarray(send_table, bf16), pltpu.HBM),
        pltpu.with_memory_space_constraint(rel_table, pltpu.HBM),
    )
    rr = shifted(send_rr, 1, 0)
    rd = shifted(send_rd, 1, -1)
    rc = shifted(send_rc, 0, -1)

    order = np.array(window_order(row_count, col_count), np.float32)
    token_lanes = np.zeros((8, count), np.float32)
    token_lanes[:2] = order.T
    grid = np.zeros((count, 8), np.float32)
    grid[:, 0] = np.arange(count) // col_count
    grid[:, 1] = np.arange(count) % col_count
    cells = cell_table(height, breadth, False)
    sent_cells = cell_table(height, breadth, True)
    cell_lanes = np.zeros((8, 128), np.float32)
    cell_lanes[:, :64] = cells.T
    cell_lanes[:, 64:] = cells.T
    rows_half = half_rows(width, channels)

    spare = np.zeros((8, up(count, 128)), np.float32)
    spare[:, :count] = token_lanes
    narrow = np.zeros((64 + FINE_PAD, 128), np.float32)
    narrow[:64, :8] = sent_cells
    narrow[64:, :8] = fine_table(height, breadth)
    small = np.concatenate(
        [differ_tables().reshape(-1, 128), narrow, *np.split(spare, spare.shape[1] // 128, 1)], 0
    )
    pair_bias, near_qkv, near_gather, near_small, near_own = expanded_bias(
        near_rel,
        qkv_weight,
        jnp.asarray(roll_gather(row_count, col_count), bf16),
        jnp.asarray(small),
        own,
    )
    scatter = jnp.asarray(unroll_scatter(row_count, col_count), bf16)
    keep, send, block = pl.pallas_call(
        functools.partial(attention_kernel, geo),
        out_shape=[
            shape((rows_half, 128), f32),
            shape((rows_half, 128), f32),
            shape((count, width), bf16),
        ],
        in_specs=[vmem] * 10 + [hbm, vmem, hbm, vmem],
        out_specs=[vmem] * 3,
        scratch_shapes=[
            pltpu.VMEM((tile_sizes(row_count, col_count)[2], width), bf16),
            pltpu.VMEM((nwin, WIN * WIN, width), bf16),
            pltpu.VMEM((nwin, WIN * WIN, width), bf16),
            pltpu.VMEM((nwin, width, WIN * WIN), bf16),
            pltpu.VMEM((nwin, width, WIN * WIN), bf16),
            pltpu.VMEM((count, width), bf16),
            pltpu.VMEM((2, nwin, WIN * WIN, 128), f32),
            pltpu.VMEM((2, rows_half, 128), f32),
            pltpu.VMEM((GROUP + 1, WIN * WIN, 128), f32),
            pltpu.VMEM((GROUP + 1, WIN * WIN, 128), f32),
            pltpu.VMEM((GROUP + 1, WIN * WIN, 128), bf16),
            pltpu.VMEM((GROUP + 1, WIN * WIN, 128), bf16),
            pltpu.VMEM(proj_weight.shape, bf16),
            pltpu.VMEM(join_block.shape, bf16),
            pltpu.SemaphoreType.DMA((2,)),
        ],
        compiler_params=pltpu.CompilerParams(vmem_limit_bytes=24 << 20),
        name="window_attention",
    )(
        near_own,
        rr,
        rc,
        rd,
        near_gather,
        ln_gain,
        ln_bias,
        near_qkv,
        qkv_bias,
        pair_bias,
        pltpu.with_memory_space_constraint(proj_weight, pltpu.HBM),
        proj_bias,
        pltpu.with_memory_space_constraint(join_block, pltpu.HBM),
        near_small,
    )

    own_b, row_b, col_b, diag_b = pl.pallas_call(
        functools.partial(back_kernel, geo),
        out_shape=[shape((size, width), bf16) for size in sizes],
        in_specs=[vmem] * 2,
        out_specs=[vmem] * 4,
        compiler_params=pltpu.CompilerParams(vmem_limit_bytes=8 << 20),
        cost_estimate=pl.CostEstimate(
            flops=2 * count * count * width, bytes_accessed=1 << 20, transcendentals=0
        ),
        name="back_pieces",
    )(block, scatter)
    rr_b = shifted(row_b, -1, 0)
    rd_b = shifted(diag_b, -1, 1)
    rc_b = shifted(col_b, 0, 1)
    mine = keep + exchanged(send, (1, 1))
    for masks in round_masks(everyone):
        mine = mine + exchanged(mine, masks)
    other = exchanged(mine, (1, 1))

    direct, share = pl.pallas_call(
        functools.partial(direct_kernel, geo),
        out_shape=[shape((count, channels), f32), shape((count, 256), bf16)],
        in_specs=[vmem] * 8,
        out_specs=[vmem] * 2,
        scratch_shapes=[pltpu.VMEM((total, width), bf16)],
        compiler_params=pltpu.CompilerParams(vmem_limit_bytes=16 << 20),
        cost_estimate=pl.CostEstimate(
            flops=2 * count * width * channels, bytes_accessed=4 << 20, transcendentals=0
        ),
        name="direct_join",
    )(
        own_b,
        rr_b,
        rc_b,
        rd_b,
        jnp.asarray(unroll_gather(row_count, col_count), bf16),
        join_block,
        jnp.asarray(grid),
        jnp.asarray(cell_lanes),
    )

    group = jnp.asarray(group_table(), bf16)
    half = pl.pallas_call(
        functools.partial(half_kernel, geo),
        out_shape=shape((cell_slots()[1], channels), f32),
        in_specs=[vmem] * 3,
        out_specs=vmem,
        scratch_shapes=[pltpu.VMEM((FINE_PAD, width // 2), f32)],
        compiler_params=pltpu.CompilerParams(vmem_limit_bytes=8 << 20),
        cost_estimate=pl.CostEstimate(
            flops=2 * 128 * width * channels, bytes_accessed=2 << 20, transcendentals=0
        ),
        name="half_join",
    )(mine, branch_weight, group)

    joined = pl.pallas_call(
        functools.partial(final_kernel, geo),
        out_shape=shape((count, channels), bf16),
        in_specs=[vmem] * 12,
        out_specs=vmem,
        scratch_shapes=[
            pltpu.VMEM((2, rows_half - NFINE * (width // 256), 128), f32),
            pltpu.VMEM((FINE_PAD, width // 2), f32),
            pltpu.VMEM((CELL_PAD, channels), f32),
            pltpu.VMEM((64, channels), f32),
        ],
        compiler_params=pltpu.CompilerParams(vmem_limit_bytes=24 << 20),
        name="final_join",
    )(
        half,
        mine,
        other,
        direct,
        share,
        branch_weight,
        branch_bias,
        join_branch,
        group,
        jnp.asarray(gram_tables(height, breadth), bf16),
        bn_gain,
        bn_bias,
    )
    return joined.reshape(row_count, col_count, channels)


def round_masks(count):
    masks = [1 << k for k in range(1, count.bit_length() - 1)]
    half = len(masks) // 2
    rounds = []
    for first, second in zip(masks[:half], masks[half : 2 * half]):
        rounds += [(second, first), (first, second)]
    return rounds + [(mask, mask) for mask in masks[2 * half :]]


def solution(mesh):
    in_specs = (P("rows", "cols", None),) + (P(),) * 13
    return jax.shard_map(
        shards, mesh=mesh, in_specs=in_specs, out_specs=P("rows", "cols", None), check_vma=False
    )
```
